128 devices in a mesh: rows: 128 (over z, x, y, core).
Axes of the slice: x: 4, y: 4, z: 4, core: 2. Of those that a mesh axis runs over, the one named last changes fastest.
Arguments:
- features: bfloat16 [131072, 1024], P('rows'), may hold values from -6 to 6
- flip_signs: int32 [131072], P('rows'), may hold values from -1 to 1, as said below
- sample_rows: int32 [4096], P('rows'), may hold values from 0 to 131071, as said below
Outputs:
- sketch: float32 [4096, 1024], P('rows')
- upper_factor: float32 [1024, 1024], replicated
- leverage: float32 [131072], P('rows')
The draws below stay inside these ranges and needn't reach their ends.
Inputs may be any that keep to these rules, and one draw needn't show every extreme that they name: `flip_signs`: every entry is -1 or 1. `sample_rows`: strictly increasing, with exactly 32 indices in each aligned block of 1024 rows; cut each such block into consecutive groups of 8 rows: every group holds at most max(1, 32 / 128) indices, and 32 / max(1, 32 / 128) groups of each block hold exactly that many.
All inputs are finite; a program needn't handle non-finite values.
Results may differ from the reference program's by a relative error of at most 0.004.
Values may be sent and summed in bfloat16 or wider, within the bound.
No kernel may reach another device: no remote copies, remote signals or barrier semaphores. Data moves between devices by JAX's collectives and lax.ppermute only.
A program may use at most 128 MiB of HBM per device.

```python
import math
import jax
import jax.numpy as jnp
from jax import lax

COLS = 1024
FACTOR = 128
ROWS_DEV = 1024
SAMPLES = 4096
ROWS = 131072
N_ROWS = 128


def draw_flip_signs(key, part):
    return (2 * jax.random.randint(jax.random.fold_in(key, 11), (ROWS,), 0, 2) - 1).astype(jnp.int32)


def draw_sample_rows(key, part):
    blocks = ROWS // ROWS_DEV
    per_block = SAMPLES // blocks
    span = ROWS_DEV // blocks
    each = max(1, per_block // blocks)
    used = per_block // each
    slice_scores = jax.random.randint(jax.random.fold_in(key, 23), (blocks, blocks), 0, 1 << 14) * blocks
    slice_scores = slice_scores + jnp.arange(blocks, dtype=jnp.int32)[None, :]
    slices = jnp.sort(jnp.argsort(slice_scores, axis=1)[:, :used], axis=1).astype(jnp.int32)
    place_scores = jax.random.randint(jax.random.fold_in(key, 29), (blocks, used, span), 0, 1 << 14) * span
    place_scores = place_scores + jnp.arange(span, dtype=jnp.int32)[None, None, :]
    within = jnp.sort(jnp.argsort(place_scores, axis=2)[:, :, :each], axis=2).astype(jnp.int32)
    picked = slices[:, :, None] * span + within + (jnp.arange(blocks, dtype=jnp.int32) * ROWS_DEV)[:, None, None]
    return picked.reshape(-1).astype(jnp.int32)


def level_of(key, shape, cuts, low, high):
    def one(position, shards_of):
        heights = jax.random.uniform(jax.random.fold_in(jax.random.fold_in(key, 6), position), (shards_of,), jnp.float32, low / len(cuts), high / len(cuts))
        return jnp.repeat(jnp.exp(heights), shape[position] // shards_of).reshape((-1,) + (1,) * (len(shape) - position - 1))

    gain = one(*cuts[0])
    for cut in cuts[1:]:
        gain = gain * one(*cut)
    return gain


def normal_values(own_key, dims, scale, limit, pieces=(), kind=jnp.bfloat16):
    entries = jax.random.normal(own_key, dims, jnp.float32) * scale
    if len(pieces) > 0:
        entries = level_of(own_key, dims, pieces, -0.22, 0.18) * entries
    return jnp.clip(entries, min=-limit, max=limit).astype(kind)


def setup_inputs(seed: int = 0) -> dict:
    keys = jax.random.split(jax.random.key(seed), 4)
    features = normal_values(keys[0], (ROWS, COLS), 1.0, 6.0, ((0, 128),))
    flip_signs = draw_flip_signs(jax.random.fold_in(keys[3], 71), 0)
    sample_rows = draw_sample_rows(jax.random.fold_in(keys[3], 71), 0)
    return {"features": features, "flip_signs": flip_signs, "sample_rows": sample_rows}


def hadamard_table(dimension):
    positions = jnp.arange(dimension, dtype=jnp.int32)
    common_bits = positions[:, None] & positions[None, :]
    parity = jnp.zeros((dimension, dimension), jnp.int32)
    for bit_pos in range(max(dimension.bit_length() - 1, 0)):
        parity = parity + (common_bits >> bit_pos & 1)
    return (1 - 2 * (parity % 2)).astype(jnp.float32)

def local_transform(row_block, sign_rows):
    flipped = row_block * sign_rows.astype(jnp.bfloat16)[:, None]
    inner_table = hadamard_table(FACTOR)
    outer_table = hadamard_table(ROWS_DEV // FACTOR)
    grouped = flipped.reshape(ROWS_DEV // FACTOR, FACTOR, COLS).astype(jnp.float32)
    section_one = jnp.einsum('ka,bac->bkc', inner_table, grouped, precision=lax.Precision.HIGHEST).astype(jnp.bfloat16)
    section_two = jnp.einsum('jb,bkc->jkc', outer_table, section_one.astype(jnp.float32), precision=lax.Precision.HIGHEST).astype(jnp.bfloat16)
    return section_two.reshape(ROWS_DEV, COLS)

def reference(features, flip_signs, sample_rows):
    blocks = features.reshape(N_ROWS, ROWS_DEV, COLS)
    sign_blocks = flip_signs.reshape(N_ROWS, ROWS_DEV)
    mixed_rows = lax.map(lambda inputs_pair: local_transform(inputs_pair[0], inputs_pair[1]), (blocks, sign_blocks))
    owner_dev = (sample_rows // ROWS_DEV).astype(jnp.int32)
    local_rows = (sample_rows % ROWS_DEV).astype(jnp.int32)
    across = hadamard_table(N_ROWS)

    def accumulate(running, source_dev):
        taken_rows = lax.dynamic_index_in_dim(mixed_rows, source_dev, 0, keepdims=False)[local_rows]
        weight_col = across[owner_dev, source_dev]
        return (running + weight_col[:, None] * taken_rows.astype(jnp.float32), None)
    running, _ = lax.scan(accumulate, jnp.zeros((SAMPLES, COLS), jnp.float32), jnp.arange(N_ROWS, dtype=jnp.int32))
    sketch = running * (1.0 / math.sqrt(SAMPLES))
    gram_matrix = jnp.dot(sketch.T, sketch, precision=lax.Precision.HIGHEST)
    lower_factor = jnp.linalg.cholesky(gram_matrix)
    upper_factor = lower_factor.T

    def block_leverage(row_block):
        solved = jax.scipy.linalg.solve_triangular(lower_factor, row_block.astype(jnp.float32).T, lower=True)
        return lax.optimization_barrier(jnp.sum(solved * solved, axis=0)) * (ROWS_DEV * N_ROWS / COLS)
    leverage = lax.map(block_leverage, blocks).reshape(-1)
    return (sketch, upper_factor, leverage)
```

```python
import functools
import math

import jax
import jax.numpy as jnp
import numpy as np
from jax import lax
from jax.experimental import pallas as pl
from jax.experimental.pallas import tpu as pltpu
from jax.sharding import PartitionSpec as P

FACTOR = 128
SAMPLES = 4096
COLS = 1024
ROWS_DEV = 1024
GROUP = 8
DEVICES = 128
CHIPS = 64
B = 128
NB = COLS // B
SB = 32
HALF_TILES = 20
SHARE = HALF_TILES * B // CHIPS
CHUNK = SHARE + GROUP
f32 = jnp.float32
bf16 = jnp.bfloat16
VMEM = pl.BlockSpec(memory_space=pltpu.VMEM)
SMEM = pl.BlockSpec(memory_space=pltpu.SMEM)


def tile_index(row, col):
    return row * NB - row * (row - 1) // 2 + col - row


def dg(a, b, ca, cb):
    return lax.dot_general(a, b, (((ca,), (cb,)), ((), ())), preferred_element_type=f32)


def split(x):
    high = x.astype(bf16)
    return high, (x - high.astype(f32)).astype(bf16)


def dot3(a, b, ca=1, cb=0):
    ah, al = split(a)
    bh, bl = split(b)
    return dg(ah, bh, ca, cb) + dg(ah, bl, ca, cb) + dg(al, bh, ca, cb)


def hadamard(dimension):
    positions = np.arange(dimension)
    common = positions[:, None] & positions[None, :]
    parity = np.zeros((dimension, dimension), np.int32)
    for bit in range(dimension.bit_length() - 1):
        parity ^= common >> bit & 1
    return (1 - 2 * parity).astype(np.float32)


def transform_kernel(x_ref, sign_ref, table_ref, rows_ref, out_ref):
    blocks = ROWS_DEV // FACTOR
    width = 256
    for lane in range(0, COLS, width):
        parts = []
        for b in range(blocks):
            signed = table_ref[...] * sign_ref[b : b + 1, :]
            inner = dg(signed.astype(bf16), x_ref[b * FACTOR : (b + 1) * FACTOR, lane : lane + width], 1, 0)
            parts.append(inner.astype(bf16).astype(f32))
        step = 1
        while step < blocks:
            parts = [
                parts[b] + parts[b ^ step] if not b & step else parts[b ^ step] - parts[b]
                for b in range(blocks)
            ]
            step *= 2
        for b in range(blocks):
            out_ref[b * FACTOR : (b + 1) * FACTOR, lane : lane + width] = parts[b].astype(bf16)
    for start in range(0, ROWS_DEV, 256):
        place = lax.broadcasted_iota(jnp.int32, (256, B), 0) + start
        hit = jnp.where(place == rows_ref[...], 1.0, 0.0).astype(bf16)
        ones = jnp.ones((B, B), bf16)
        out_ref[start : start + 256, COLS:] = dg(hit, ones, 1, 0).astype(bf16)


def transform(features, signs, local_rows):
    rows = jnp.concatenate([local_rows, jnp.full((B - local_rows.shape[0],), -1, jnp.int32)])[None, :]
    return pl.pallas_call(
        transform_kernel,
        out_shape=jax.ShapeDtypeStruct((ROWS_DEV, COLS + B), bf16),
        in_specs=[VMEM] * 4,
        out_specs=VMEM,
        compiler_params=pltpu.CompilerParams(vmem_limit_bytes=40 << 20),
        name="transform",
    )(features, signs.astype(f32).reshape(ROWS_DEV // FACTOR, FACTOR), jnp.asarray(hadamard(FACTOR)), rows)


def combine_kernel(core_ref, p_ref, table_ref, block_ref, mine_ref, other_ref, x_ref):
    core = core_ref[0]
    mask = p_ref[:, COLS:].astype(f32)
    row = lax.broadcasted_iota(jnp.int32, (ROWS_DEV, B), 0)
    lane = lax.broadcasted_iota(jnp.int32, (ROWS_DEV, B), 1)
    mask = jnp.where((row & (GROUP - 1)) == (lane & (GROUP - 1)), mask, 0.0).astype(bf16)
    pick = dg(block_ref[...], mask, 1, 0).astype(bf16)
    mixer = table_ref[...] * jnp.concatenate([pick] * GROUP, axis=1)
    rows = dg(mixer, p_ref[:, :COLS], 1, 0) * (1.0 / math.sqrt(SAMPLES))
    for b in range(NB):
        for half in range(2):
            x_ref[pl.ds(half * CHIPS * CHUNK + SHARE + b, CHIPS, stride=CHUNK), :] = rows[
                half * CHIPS : (half + 1) * CHIPS, b * B : (b + 1) * B
            ]
    high, low = split(rows)
    for r in range(NB):
        left_high, left_low = high[:, r * B : (r + 1) * B], low[:, r * B : (r + 1) * B]
        right_high, right_low = high[:, r * B :], low[:, r * B :]
        gram = dg(left_high, right_high, 0, 0) + dg(left_high, right_low, 0, 0) + dg(left_low, right_high, 0, 0)
        for c in range(r, NB):
            half, spot = divmod(tile_index(r, c), HALF_TILES)
            tile = gram[:, (c - r) * B : (c - r + 1) * B]
            put_rows(x_ref, half, spot * B, tile)
    for t in range(NB * (NB + 1) // 2, 2 * HALF_TILES):
        half, spot = divmod(t, HALF_TILES)
        put_rows(x_ref, half, spot * B, jnp.zeros((B, B), f32))
    size = CHIPS * CHUNK
    mine_ref[...] = x_ref[pl.ds(pl.multiple_of(core * size, 8), size), :]
    other_ref[...] = x_ref[pl.ds(pl.multiple_of((1 - core) * size, 8), size), :]


def put_rows(x_ref, half, start, tile):
    done = 0
    while done < B:
        chip, spot = divmod(start + done, SHARE)
        count = min(SHARE - spot, B - done)
        base = (half * CHIPS + chip) * CHUNK + spot
        x_ref[base : base + count, :] = tile[done : done + count, :]
        done += count


def combine(core, pieces):
    order = np.concatenate([np.arange(0, DEVICES, 2), np.arange(1, DEVICES, 2)])
    table = np.repeat(hadamard(DEVICES)[order], GROUP, axis=1)
    block = np.repeat(np.eye(DEVICES, dtype=np.float32)[order], GROUP, axis=1)
    shape = jax.ShapeDtypeStruct((CHIPS * CHUNK, B), f32)
    return pl.pallas_call(
        combine_kernel,
        out_shape=(shape, shape),
        in_specs=[SMEM, VMEM, VMEM, VMEM],
        out_specs=(VMEM, VMEM),
        scratch_shapes=[pltpu.VMEM((2 * CHIPS * CHUNK, B), f32)],
        compiler_params=pltpu.CompilerParams(vmem_limit_bytes=40 << 20),
        name="combine",
    )(core, pieces, jnp.asarray(table, bf16), jnp.asarray(block, bf16))


def factor_rows(R, lane0, w):
    rid = lax.broadcasted_iota(jnp.int32, (SB, B), 0)
    scale = jnp.ones((SB, B), f32)
    for k in range(SB):
        col = jnp.broadcast_to(R[:, lane0 + k : lane0 + k + 1], (SB, B))
        piv = col[k : k + 1, :]
        inv = 1.0 / piv
        scale = jnp.where(rid == k, jnp.broadcast_to(lax.rsqrt(piv), (SB, B)), scale)
        mult = jnp.where(rid > k, col * inv, 0.0)
        row = jnp.broadcast_to(R[k : k + 1, :], (SB, w))
        R = R - jnp.concatenate([mult] * (w // B), axis=1) * row
    return R * jnp.concatenate([scale] * (w // B), axis=1)


def factor_kernel(meta_ref, mine_ref, other_ref, rows_ref, f_ref, u_ref, lev_ref, sk_ref, a_ref, s_ref, x_ref, acc_ref):
    core = meta_ref[0]
    for k in range(SAMPLES // DEVICES):
        q = meta_ref[1 + k] // GROUP
        spot = jnp.bitwise_xor(q % 2, core)
        sk_ref[k] = rows_ref[q // 2, pl.ds(pl.multiple_of(spot * GROUP, GROUP), GROUP), :]
    first = core == 0
    for r in range(NB):
        for c in range(r, NB):
            half, spot = divmod(tile_index(r, c), HALF_TILES)
            own = mine_ref[spot * B : (spot + 1) * B, :]
            far = other_ref[spot * B : (spot + 1) * B, :]
            a_ref[r * B : (r + 1) * B, c * B : (c + 1) * B] = jnp.where(first == (half == 0), own, far)
    u_ref[...] = jnp.zeros_like(u_ref)
    x_ref[...] = jnp.zeros_like(x_ref)
    acc_ref[...] = jnp.zeros_like(acc_ref)
    ri = lax.broadcasted_iota(jnp.int32, (B, B), 0)
    ci = lax.broadcasted_iota(jnp.int32, (B, B), 1)

    def panel(p, _):
        o = pl.multiple_of(p * B, B)
        s_ref[:, :B] = a_ref[pl.ds(o, B), pl.ds(o, B)]
        s_ref[:, B:] = jnp.where(ri == ci, 1.0, 0.0).astype(f32)
        for i in range(B // SB):
            R = factor_rows(s_ref[i * SB : (i + 1) * SB, :], i * SB, 2 * B)
            s_ref[i * SB : (i + 1) * SB, :] = R
            if i < B // SB - 1:
                update = dot3(R[:, :B], R, 0, 0)
                s_ref[(i + 1) * SB :, :] = s_ref[(i + 1) * SB :, :] - update[(i + 1) * SB :, :]
        inverse = jnp.where(ri >= ci, s_ref[:, B:], 0.0)
        u_ref[pl.ds(o, B), pl.ds(o, B)] = jnp.where(ri <= ci, s_ref[:, :B], 0.0)

        def across(q, _):
            oq = pl.multiple_of(q * B, B)
            u_ref[pl.ds(o, B), pl.ds(oq, B)] = dot3(inverse, a_ref[pl.ds(o, B), pl.ds(oq, B)])
            return 0

        lax.fori_loop(p + 1, NB, across, 0)

        def trail(q, _):
            oq = pl.multiple_of(q * B, B)
            a_ref[pl.ds(oq, B), :] = a_ref[pl.ds(oq, B), :] - dot3(u_ref[pl.ds(o, B), pl.ds(oq, B)], u_ref[pl.ds(o, B), :], 0, 0)
            return 0

        lax.fori_loop(p + 1, NB, trail, 0)
        above = lax.broadcasted_iota(jnp.int32, (COLS, B), 0) < o
        ucol = jnp.where(above, u_ref[:, pl.ds(o, B)], 0.0)
        x_ref[:, pl.ds(o, B)] = -dot3(dot3(x_ref[...], ucol), inverse, 1, 1)
        x_ref[pl.ds(o, B), pl.ds(o, B)] = inverse.T
        high, low = split(x_ref[:, pl.ds(o, B)])
        w = dg(f_ref[...], high, 1, 0) + dg(f_ref[...], low, 1, 0)
        acc_ref[...] += w * w
        return 0

    lax.fori_loop(0, NB, panel, 0)
    lev_ref[...] = lax.dot_general(
        jnp.full((8, B), float(DEVICES * ROWS_DEV // COLS), f32),
        acc_ref[...],
        (((1,), (1,)), ((), ())),
        precision=lax.Precision.HIGHEST,
        preferred_element_type=f32,
    )


def factor(meta, mine, other, rows, features):
    return pl.pallas_call(
        factor_kernel,
        out_shape=(
            jax.ShapeDtypeStruct((COLS, COLS), f32),
            jax.ShapeDtypeStruct((8, ROWS_DEV), f32),
            jax.ShapeDtypeStruct((SAMPLES // DEVICES, GROUP, B), f32),
        ),
        in_specs=[SMEM] + [VMEM] * 4,
        out_specs=(VMEM,) * 3,
        scratch_shapes=[
            pltpu.VMEM((COLS, COLS), f32),
            pltpu.VMEM((B, 2 * B), f32),
            pltpu.VMEM((COLS, COLS), f32),
            pltpu.VMEM((ROWS_DEV, B), f32),
        ],
        compiler_params=pltpu.CompilerParams(vmem_limit_bytes=60 << 20),
        name="factor",
    )(meta, mine, other, rows, features)


def shards(features, flip_signs, sample_rows):
    position = lax.axis_index("rows")
    core = position % 2
    local_rows = sample_rows - position * ROWS_DEV
    mixed = transform(features, flip_signs, local_rows)
    pieces = lax.all_to_all(
        mixed.reshape(DEVICES, GROUP, COLS + B), "rows", split_axis=0, concat_axis=0, tiled=True
    ).reshape(ROWS_DEV, COLS + B)
    mine, other = combine(core[None], pieces)
    swap = [(d, d ^ 1) for d in range(DEVICES)]
    came = lax.ppermute(other, "rows", swap).reshape(CHIPS, CHUNK, B)
    mine = mine.reshape(CHIPS, CHUNK, B)
    shares = jnp.concatenate([mine[:, :SHARE] + came[:, :SHARE], mine[:, SHARE:], came[:, SHARE:]], axis=1)
    same_core = [list(range(c, DEVICES, 2)) for c in range(2)]
    got = lax.all_to_all(
        shares, "rows", split_axis=0, concat_axis=0, tiled=True, axis_index_groups=same_core
    )
    total = jnp.sum(got[:, :SHARE], axis=0)
    half = lax.all_to_all(
        jnp.broadcast_to(total[None], (CHIPS, SHARE, B)),
        "rows", split_axis=0, concat_axis=0, tiled=True, axis_index_groups=same_core,
    ).reshape(HALF_TILES * B, B)
    far = lax.ppermute(half, "rows", swap)
    meta = jnp.concatenate([core[None], local_rows])
    upper, lev, sketch = factor(meta, half, far, got[:, SHARE:], features)
    return sketch.reshape(-1, COLS), upper, lev[0]


def solution(mesh):
    placed = (P("rows", None), P("rows"), P("rows"))
    return jax.shard_map(
        shards,
        mesh=mesh,
        in_specs=placed,
        out_specs=(P("rows", None), P(), P("rows")),
        check_vma=False,
    )
```

```python
import math

import jax
import jax.numpy as jnp
import numpy as np
from jax import lax
from jax.experimental import pallas as pl
from jax.experimental.pallas import tpu as pltpu
from jax.sharding import PartitionSpec as P

FACTOR = 128
SAMPLES = 4096
COLS = 1024
ROWS_DEV = 1024
GROUP = 8
DEVICES = 128
CHIPS = 64
B = 128
NB = COLS // B
SB = 32
HALF_TILES = 20
SHARE = HALF_TILES * B // CHIPS
CHUNK = SHARE + GROUP
f32 = jnp.float32
bf16 = jnp.bfloat16
VMEM = pl.BlockSpec(memory_space=pltpu.VMEM)
SMEM = pl.BlockSpec(memory_space=pltpu.SMEM)


def tile_index(row, col):
    return row * NB - row * (row - 1) // 2 + col - row


def dg(a, b, ca, cb):
    return lax.dot_general(a, b, (((ca,), (cb,)), ((), ())), preferred_element_type=f32)


def split(x):
    high = x.astype(bf16)
    return high, (x - high.astype(f32)).astype(bf16)


def dot3s(a, b, ca=1, cb=0):
    (ah, al), (bh, bl) = a, b
    return dg(ah, bh, ca, cb) + dg(ah, bl, ca, cb) + dg(al, bh, ca, cb)


def dot3(a, b, ca=1, cb=0):
    return dot3s(split(a), split(b), ca, cb)


def hadamard(dimension):
    positions = np.arange(dimension)
    common = positions[:, None] & positions[None, :]
    parity = np.zeros((dimension, dimension), np.int32)
    for bit in range(dimension.bit_length() - 1):
        parity ^= common >> bit & 1
    return (1 - 2 * parity).astype(np.float32)


def transform_kernel(x_ref, sign_ref, table_ref, rows_ref, out_ref):
    blocks = ROWS_DEV // FACTOR
    width = 256
    for lane in range(0, COLS, width):
        parts = []
        for b in range(blocks):
            signed = table_ref[...] * sign_ref[b : b + 1, :]
            inner = dg(signed.astype(bf16), x_ref[b * FACTOR : (b + 1) * FACTOR, lane : lane + width], 1, 0)
            parts.append(inner.astype(bf16).astype(f32))
        step = 1
        while step < blocks:
            parts = [
                parts[b] + parts[b ^ step] if not b & step else parts[b ^ step] - parts[b]
                for b in range(blocks)
            ]
            step *= 2
        for b in range(blocks):
            out_ref[b * FACTOR : (b + 1) * FACTOR, lane : lane + width] = parts[b].astype(bf16)
    for start in range(0, ROWS_DEV, 256):
        place = lax.broadcasted_iota(jnp.int32, (256, B), 0) + start
        hit = jnp.where(place == rows_ref[...], 1.0, 0.0).astype(bf16)
        ones = jnp.ones((B, B), bf16)
        out_ref[start : start + 256, COLS:] = dg(hit, ones, 1, 0).astype(bf16)


def transform(features, signs, local_rows):
    rows = jnp.concatenate([local_rows, jnp.full((B - local_rows.shape[0],), -1, jnp.int32)])[None, :]
    return pl.pallas_call(
        transform_kernel,
        out_shape=jax.ShapeDtypeStruct((ROWS_DEV, COLS + B), bf16),
        in_specs=[VMEM] * 4,
        out_specs=VMEM,
        compiler_params=pltpu.CompilerParams(vmem_limit_bytes=40 << 20),
        name="transform",
    )(features, signs.astype(f32).reshape(ROWS_DEV // FACTOR, FACTOR), jnp.asarray(hadamard(FACTOR)), rows)


def combine_kernel(core_ref, p_ref, table_ref, block_ref, mine_ref, other_ref, x_ref):
    core = core_ref[0]
    mask = p_ref[:, COLS:].astype(f32)
    row = lax.broadcasted_iota(jnp.int32, (ROWS_DEV, B), 0)
    lane = lax.broadcasted_iota(jnp.int32, (ROWS_DEV, B), 1)
    mask = jnp.where((row & (GROUP - 1)) == (lane & (GROUP - 1)), mask, 0.0).astype(bf16)
    pick = dg(block_ref[...], mask, 1, 0).astype(bf16)
    mixer = table_ref[...] * jnp.concatenate([pick] * GROUP, axis=1)
    rows = dg(mixer, p_ref[:, :COLS], 1, 0) * (1.0 / math.sqrt(SAMPLES))
    for b in range(NB):
        for half in range(2):
            x_ref[pl.ds(half * CHIPS * CHUNK + SHARE + b, CHIPS, stride=CHUNK), :] = rows[
                half * CHIPS : (half + 1) * CHIPS, b * B : (b + 1) * B
            ]
    high, low = split(rows)
    for r in range(NB):
        left_high, left_low = high[:, r * B : (r + 1) * B], low[:, r * B : (r + 1) * B]
        right_high, right_low = high[:, r * B :], low[:, r * B :]
        gram = dg(left_high, right_high, 0, 0) + dg(left_high, right_low, 0, 0) + dg(left_low, right_high, 0, 0)
        for c in range(r, NB):
            half, spot = divmod(tile_index(r, c), HALF_TILES)
            tile = gram[:, (c - r) * B : (c - r + 1) * B]
            put_rows(x_ref, half, spot * B, tile)
    for t in range(NB * (NB + 1) // 2, 2 * HALF_TILES):
        half, spot = divmod(t, HALF_TILES)
        put_rows(x_ref, half, spot * B, jnp.zeros((B, B), f32))
    size = CHIPS * CHUNK
    mine_ref[...] = x_ref[pl.ds(pl.multiple_of(core * size, 8), size), :]
    other_ref[...] = x_ref[pl.ds(pl.multiple_of((1 - core) * size, 8), size), :]


def put_rows(x_ref, half, start, tile):
    done = 0
    while done < B:
        chip, spot = divmod(start + done, SHARE)
        count = min(SHARE - spot, B - done)
        base = (half * CHIPS + chip) * CHUNK + spot
        x_ref[base : base + count, :] = tile[done : done + count, :]
        done += count


def combine(core, pieces):
    order = np.concatenate([np.arange(0, DEVICES, 2), np.arange(1, DEVICES, 2)])
    table = np.repeat(hadamard(DEVICES)[order], GROUP, axis=1)
    block = np.repeat(np.eye(DEVICES, dtype=np.float32)[order], GROUP, axis=1)
    shape = jax.ShapeDtypeStruct((CHIPS * CHUNK, B), f32)
    return pl.pallas_call(
        combine_kernel,
        out_shape=(shape, shape),
        in_specs=[SMEM, VMEM, VMEM, VMEM],
        out_specs=(VMEM, VMEM),
        scratch_shapes=[pltpu.VMEM((2 * CHIPS * CHUNK, B), f32)],
        compiler_params=pltpu.CompilerParams(vmem_limit_bytes=40 << 20),
        name="combine",
    )(core, pieces, jnp.asarray(table, bf16), jnp.asarray(block, bf16))


def factor_rows(s_ref, i):
    groups = SB // 8
    rid = lax.broadcasted_iota(jnp.int32, (8, B), 0)
    base = i * SB
    R = [[s_ref[base + 8 * v : base + 8 * v + 8, h * B : (h + 1) * B] for h in range(2)] for v in range(groups)]

    def spread(x, k):
        return jnp.broadcast_to(x[k : k + 1, :], (8, B))

    for g in range(groups):
        lane = base + 8 * g
        rest = range(groups - g)
        C = [[jnp.broadcast_to(R[g + v][0][:, lane + k : lane + k + 1], (8, B)) for v in rest] for k in range(8)]
        scale = None
        for k in range(8):
            pivot = spread(C[k][0], k)
            inverse = 1.0 / pivot
            factors = [C[k][v] * inverse for v in rest]
            factors[0] = jnp.where(rid > k, factors[0], 0.0)
            for j in range(k + 1, 8):
                row = spread(C[j][0], k)
                for v in rest:
                    C[j][v] = C[j][v] - factors[v] * row
            for h in range(2):
                row = spread(R[g][h], k)
                for v in rest:
                    R[g + v][h] = R[g + v][h] - factors[v] * row
            root = lax.rsqrt(pivot)
            scale = root if scale is None else jnp.where(rid >= k, root, scale)
        for h in range(2):
            R[g][h] = R[g][h] * scale
    for v in range(groups):
        for h in range(2):
            s_ref[base + 8 * v : base + 8 * v + 8, h * B : (h + 1) * B] = R[v][h]


def finish_panel(p, f_ref, u_ref, a_ref, s_ref, uh_ref, ul_ref, xh_ref, xl_ref, acc_ref):
    o = p * B
    e = o + B
    ri = lax.broadcasted_iota(jnp.int32, (B, B), 0)
    ci = lax.broadcasted_iota(jnp.int32, (B, B), 1)
    inverse = jnp.where(ri >= ci, s_ref[:, B:], 0.0)
    u_ref[o:e, o:e] = jnp.where(ri <= ci, s_ref[:, :B], 0.0)
    if e < COLS:
        across = dot3s(split(inverse), split(a_ref[o:e, e:]))
        u_ref[o:e, e:] = across
        high, low = split(across)
        uh_ref[o:e, e:] = high
        ul_ref[o:e, e:] = low
        for q in range(p + 1, NB):
            c = q * B - e
            left = jnp.concatenate([high[:, c : c + B], high[:, c : c + B], low[:, c : c + B]], axis=0)
            right = jnp.concatenate([high[:, c:], low[:, c:], high[:, c:]], axis=0)
            a_ref[q * B : (q + 1) * B, q * B :] -= dg(left, right, 0, 0)
    corner = split(inverse.T)
    if p > 0:
        above = dot3s((xh_ref[:o, :o], xl_ref[:o, :o]), (uh_ref[:o, o:e], ul_ref[:o, o:e]))
        xh_ref[:o, o:e], xl_ref[:o, o:e] = split(-dot3s(split(above), corner))
    xh_ref[o:e, o:e], xl_ref[o:e, o:e] = corner
    if e < COLS:
        xh_ref[e:, o:e] = jnp.zeros((COLS - e, B), bf16)
        xl_ref[e:, o:e] = jnp.zeros((COLS - e, B), bf16)
    if p % 2:
        pair = slice(o - B, e)
        w = dg(f_ref[:, :e], xh_ref[:e, pair], 1, 0) + dg(f_ref[:, :e], xl_ref[:e, pair], 1, 0)
        acc_ref[...] += w * w


def factor_kernel(
    meta_ref, mine_ref, other_ref, rows_ref, f_ref, u_ref, lev_ref, sk_ref,
    a_ref, s_ref, uh_ref, ul_ref, xh_ref, xl_ref, acc_ref,
):
    core = meta_ref[0]
    for k in range(SAMPLES // DEVICES):
        q = meta_ref[1 + k] // GROUP
        spot = jnp.bitwise_xor(q % 2, core)
        sk_ref[k] = rows_ref[q // 2, pl.ds(pl.multiple_of(spot * GROUP, GROUP), GROUP), :]
    first = core == 0
    for r in range(NB):
        for c in range(r, NB):
            half, spot = divmod(tile_index(r, c), HALF_TILES)
            own = mine_ref[spot * B : (spot + 1) * B, :]
            far = other_ref[spot * B : (spot + 1) * B, :]
            a_ref[r * B : (r + 1) * B, c * B : (c + 1) * B] = jnp.where(first == (half == 0), own, far)
    u_ref[...] = jnp.zeros_like(u_ref)
    acc_ref[...] = jnp.zeros_like(acc_ref)
    ri = lax.broadcasted_iota(jnp.int32, (B, B), 0)
    ci = lax.broadcasted_iota(jnp.int32, (B, B), 1)

    def panel(p, _):
        o = pl.multiple_of(p * B, B)
        s_ref[:, :B] = a_ref[pl.ds(o, B), pl.ds(o, B)]
        s_ref[:, B:] = jnp.where(ri == ci, 1.0, 0.0).astype(f32)
        for i in range(B // SB):
            factor_rows(s_ref, i)
            if i < B // SB - 1:
                R = s_ref[i * SB : (i + 1) * SB, :]
                update = dot3(R[:, :B], R, 0, 0)
                s_ref[(i + 1) * SB :, :] = s_ref[(i + 1) * SB :, :] - update[(i + 1) * SB :, :]
        for static in range(NB):

            @pl.when(p == static)
            def _():
                finish_panel(static, f_ref, u_ref, a_ref, s_ref, uh_ref, ul_ref, xh_ref, xl_ref, acc_ref)

        return 0

    lax.fori_loop(0, NB, panel, 0)
    high, low = split(acc_ref[...])
    weight = jnp.full((8, 2 * B), float(DEVICES * ROWS_DEV // COLS), bf16)
    lev_ref[...] = dg(weight, high, 1, 1) + dg(weight, low, 1, 1)


def factor(meta, mine, other, rows, features):
    return pl.pallas_call(
        factor_kernel,
        out_shape=(
            jax.ShapeDtypeStruct((COLS, COLS), f32),
            jax.ShapeDtypeStruct((8, ROWS_DEV), f32),
            jax.ShapeDtypeStruct((SAMPLES // DEVICES, GROUP, B), f32),
        ),
        in_specs=[SMEM] + [VMEM] * 4,
        out_specs=(VMEM,) * 3,
        scratch_shapes=[pltpu.VMEM((COLS, COLS), f32), pltpu.VMEM((B, 2 * B), f32)]
        + [pltpu.VMEM((COLS, COLS), bf16)] * 4
        + [pltpu.VMEM((ROWS_DEV, 2 * B), f32)],
        compiler_params=pltpu.CompilerParams(vmem_limit_bytes=60 << 20),
        name="factor",
    )(meta, mine, other, rows, features)


def shards(features, flip_signs, sample_rows):
    position = lax.axis_index("rows")
    core = position % 2
    local_rows = sample_rows - position * ROWS_DEV
    mixed = transform(features, flip_signs, local_rows)
    pieces = lax.all_to_all(
        mixed.reshape(DEVICES, GROUP, COLS + B), "rows", split_axis=0, concat_axis=0, tiled=True
    ).reshape(ROWS_DEV, COLS + B)
    mine, other = combine(core[None], pieces)
    swap = [(d, d ^ 1) for d in range(DEVICES)]
    came = lax.ppermute(other, "rows", swap).reshape(CHIPS, CHUNK, B)
    mine = mine.reshape(CHIPS, CHUNK, B)
    shares = jnp.concatenate([mine[:, :SHARE] + came[:, :SHARE], mine[:, SHARE:], came[:, SHARE:]], axis=1)
    same_core = [list(range(c, DEVICES, 2)) for c in range(2)]
    got = lax.all_to_all(
        shares, "rows", split_axis=0, concat_axis=0, tiled=True, axis_index_groups=same_core
    )
    total = jnp.sum(got[:, :SHARE], axis=0)
    half = lax.all_to_all(
        jnp.broadcast_to(total[None], (CHIPS, SHARE, B)),
        "rows", split_axis=0, concat_axis=0, tiled=True, axis_index_groups=same_core,
    ).reshape(HALF_TILES * B, B)
    far = lax.ppermute(half, "rows", swap)
    meta = jnp.concatenate([core[None], local_rows])
    upper, lev, sketch = factor(meta, half, far, got[:, SHARE:], features)
    return sketch.reshape(-1, COLS), upper, lev[0]


def solution(mesh):
    placed = (P("rows", None), P("rows"), P("rows"))
    return jax.shard_map(
        shards,
        mesh=mesh,
        in_specs=placed,
        out_specs=(P("rows", None), P(), P("rows")),
        check_vma=False,
    )
```

```python
import math

import jax
import jax.numpy as jnp
import numpy as np
from jax import lax
from jax.experimental import pallas as pl
from jax.experimental.pallas import tpu as pltpu
from jax.sharding import PartitionSpec as P

FACTOR = 128
SAMPLES = 4096
COLS = 1024
ROWS_DEV = 1024
GROUP = 8
DEVICES = 128
CHIPS = 64
B = 128
NB = COLS // B
SB = 32
HALF_TILES = 20
SHARE = HALF_TILES * B // CHIPS
CHUNK = SHARE + GROUP
f32 = jnp.float32
bf16 = jnp.bfloat16
ANY = pl.BlockSpec(memory_space=pl.ANY)
VMEM = pl.BlockSpec(memory_space=pltpu.VMEM)
SMEM = pl.BlockSpec(memory_space=pltpu.SMEM)


def tile_index(row, col):
    return row * NB - row * (row - 1) // 2 + col - row


def dg(a, b, ca, cb):
    return lax.dot_general(a, b, (((ca,), (cb,)), ((), ())), preferred_element_type=f32)


def split(x):
    high = x.astype(bf16)
    return high, (x - high.astype(f32)).astype(bf16)


def dot3s(a, b, ca=1, cb=0):
    (ah, al), (bh, bl) = a, b
    return dg(ah, bh, ca, cb) + dg(ah, bl, ca, cb) + dg(al, bh, ca, cb)


def dot3(a, b, ca=1, cb=0):
    return dot3s(split(a), split(b), ca, cb)


def hadamard(dimension):
    positions = np.arange(dimension)
    common = positions[:, None] & positions[None, :]
    parity = np.zeros((dimension, dimension), np.int32)
    for bit in range(dimension.bit_length() - 1):
        parity ^= common >> bit & 1
    return (1 - 2 * parity).astype(np.float32)


def transform_kernel(x_hbm, sign_ref, rows_ref, table_ref, out_hbm, x_ref, out_ref, in_sem, out_sem):
    blocks = ROWS_DEV // FACTOR
    width = 256
    parts = COLS // width

    def fetch(c):
        lanes = pl.ds(c * width, width)
        return pltpu.make_async_copy(x_hbm.at[:, lanes], x_ref.at[:, lanes], in_sem.at[c])

    def put(c):
        lanes = pl.ds(c * width, width) if c < parts else pl.ds(COLS, B)
        return pltpu.make_async_copy(out_ref.at[:, lanes], out_hbm.at[:, lanes], out_sem.at[c])

    for c in range(parts):
        fetch(c).start()
    sampled = rows_ref[...] & (ROWS_DEV - 1)
    ones = jnp.ones((sampled.shape[1], B), bf16)
    for start in range(0, ROWS_DEV, 256):
        place = lax.broadcasted_iota(jnp.int32, (256, sampled.shape[1]), 0) + start
        hit = jnp.where(place == sampled, 1.0, 0.0).astype(bf16)
        out_ref[start : start + 256, COLS:] = dg(hit, ones, 1, 0).astype(bf16)
    put(parts).start()
    signs = sign_ref[...].astype(f32)
    tables = [(table_ref[...] * signs[b : b + 1, :]).astype(bf16) for b in range(blocks)]
    for c in range(parts):
        fetch(c).wait()
        lanes = slice(c * width, (c + 1) * width)
        mixed = []
        for b in range(blocks):
            inner = dg(tables[b], x_ref[b * FACTOR : (b + 1) * FACTOR, lanes], 1, 0)
            mixed.append(inner.astype(bf16).astype(f32))
        step = 1
        while step < blocks:
            mixed = [
                mixed[b] + mixed[b ^ step] if not b & step else mixed[b ^ step] - mixed[b]
                for b in range(blocks)
            ]
            step *= 2
        for b in range(blocks):
            out_ref[b * FACTOR : (b + 1) * FACTOR, lanes] = mixed[b].astype(bf16)
        put(c).start()
    for c in range(parts + 1):
        put(c).wait()


def transform(features, flip_signs, sample_rows):
    parts = COLS // 256
    return pl.pallas_call(
        transform_kernel,
        out_shape=jax.ShapeDtypeStruct((ROWS_DEV, COLS + B), bf16),
        in_specs=[ANY] + [VMEM] * 3,
        out_specs=ANY,
        scratch_shapes=[
            pltpu.VMEM((ROWS_DEV, COLS), bf16),
            pltpu.VMEM((ROWS_DEV, COLS + B), bf16),
            pltpu.SemaphoreType.DMA((parts,)),
            pltpu.SemaphoreType.DMA((parts + 1,)),
        ],
        compiler_params=pltpu.CompilerParams(vmem_limit_bytes=16 << 20),
        name="transform",
    )(
        features,
        flip_signs.reshape(ROWS_DEV // FACTOR, FACTOR),
        sample_rows.reshape(1, -1),
        jnp.asarray(hadamard(FACTOR)),
    )


def combine_kernel(p_ref, table_ref, block_ref, mine_ref, other_ref, x_ref):
    core = lax.axis_index("rows") % 2
    mask = p_ref[:, COLS:].astype(f32)
    row = lax.broadcasted_iota(jnp.int32, (ROWS_DEV, B), 0)
    lane = lax.broadcasted_iota(jnp.int32, (ROWS_DEV, B), 1)
    mask = jnp.where((row & (GROUP - 1)) == (lane & (GROUP - 1)), mask, 0.0).astype(bf16)
    pick = dg(block_ref[...], mask, 1, 0).astype(bf16)
    mixer = table_ref[...] * jnp.concatenate([pick] * GROUP, axis=1)
    rows = dg(mixer, p_ref[:, :COLS], 1, 0) * (1.0 / math.sqrt(SAMPLES))
    for b in range(NB):
        for half in range(2):
            x_ref[pl.ds(half * CHIPS * CHUNK + SHARE + b, CHIPS, stride=CHUNK), :] = rows[
                half * CHIPS : (half + 1) * CHIPS, b * B : (b + 1) * B
            ]
    high, low = split(rows)
    for r in range(NB):
        left_high, left_low = high[:, r * B : (r + 1) * B], low[:, r * B : (r + 1) * B]
        right_high, right_low = high[:, r * B :], low[:, r * B :]
        gram = dg(left_high, right_high, 0, 0) + dg(left_high, right_low, 0, 0) + dg(left_low, right_high, 0, 0)
        for c in range(r, NB):
            half, spot = divmod(tile_index(r, c), HALF_TILES)
            tile = gram[:, (c - r) * B : (c - r + 1) * B]
            put_rows(x_ref, half, spot * B, tile)
    for t in range(NB * (NB + 1) // 2, 2 * HALF_TILES):
        half, spot = divmod(t, HALF_TILES)
        put_rows(x_ref, half, spot * B, jnp.zeros((B, B), f32))
    size = CHIPS * CHUNK
    mine_ref[...] = x_ref[pl.ds(pl.multiple_of(core * size, 8), size), :]
    other_ref[...] = x_ref[pl.ds(pl.multiple_of((1 - core) * size, 8), size), :]


def put_rows(x_ref, half, start, tile):
    done = 0
    while done < B:
        chip, spot = divmod(start + done, SHARE)
        count = min(SHARE - spot, B - done)
        base = (half * CHIPS + chip) * CHUNK + spot
        x_ref[base : base + count, :] = tile[done : done + count, :]
        done += count


def combine(pieces):
    order = np.concatenate([np.arange(0, DEVICES, 2), np.arange(1, DEVICES, 2)])
    table = np.repeat(hadamard(DEVICES)[order], GROUP, axis=1)
    block = np.repeat(np.eye(DEVICES, dtype=np.float32)[order], GROUP, axis=1)
    shape = jax.ShapeDtypeStruct((CHIPS * CHUNK, B), f32)
    return pl.pallas_call(
        combine_kernel,
        out_shape=(shape, shape),
        in_specs=[VMEM] * 3,
        out_specs=(VMEM, VMEM),
        scratch_shapes=[pltpu.VMEM((2 * CHIPS * CHUNK, B), f32)],
        compiler_params=pltpu.CompilerParams(vmem_limit_bytes=24 << 20),
        name="combine",
    )(pieces, jnp.asarray(table, bf16), jnp.asarray(block, bf16))


def factor_rows(s_ref, i):
    groups = SB // 8
    rid = lax.broadcasted_iota(jnp.int32, (8, B), 0)
    base = i * SB
    R = [[s_ref[base + 8 * v : base + 8 * v + 8, h * B : (h + 1) * B] for h in range(2)] for v in range(groups)]

    def spread(x, k):
        return jnp.broadcast_to(x[k : k + 1, :], (8, B))

    for g in range(groups):
        lane = base + 8 * g
        rest = range(groups - g)
        C = [[jnp.broadcast_to(R[g + v][0][:, lane + k : lane + k + 1], (8, B)) for v in rest] for k in range(8)]
        scale = None
        for k in range(8):
            pivot = spread(C[k][0], k)
            inverse = 1.0 / pivot
            factors = [C[k][v] * inverse for v in rest]
            factors[0] = jnp.where(rid > k, factors[0], 0.0)
            for j in range(k + 1, 8):
                row = spread(C[j][0], k)
                for v in rest:
                    C[j][v] = C[j][v] - factors[v] * row
            for h in range(2):
                row = spread(R[g][h], k)
                for v in rest:
                    R[g + v][h] = R[g + v][h] - factors[v] * row
            root = lax.rsqrt(pivot)
            scale = root if scale is None else jnp.where(rid >= k, root, scale)
        for h in range(2):
            R[g][h] = R[g][h] * scale
    for v in range(groups):
        for h in range(2):
            s_ref[base + 8 * v : base + 8 * v + 8, h * B : (h + 1) * B] = R[v][h]


def finish_panel(p, load, store, f_ref, u_ref, a_ref, s_ref, uh_ref, ul_ref, xh_ref, xl_ref, acc_ref):
    o = p * B
    e = o + B
    ri = lax.broadcasted_iota(jnp.int32, (B, B), 0)
    ci = lax.broadcasted_iota(jnp.int32, (B, B), 1)
    inverse = jnp.where(ri >= ci, s_ref[:, B:], 0.0)
    u_ref[o:e, o:e] = jnp.where(ri <= ci, s_ref[:, :B], 0.0)
    if e < COLS:
        across = dot3s(split(inverse), split(a_ref[o:e, e:]))
        u_ref[o:e, e:] = across
        high, low = split(across)
        uh_ref[o:e, e:] = high
        ul_ref[o:e, e:] = low
        for q in range(p + 1, NB):
            c = q * B - e
            left = jnp.concatenate([high[:, c : c + B], high[:, c : c + B], low[:, c : c + B]], axis=0)
            right = jnp.concatenate([high[:, c:], low[:, c:], high[:, c:]], axis=0)
            a_ref[q * B : (q + 1) * B, q * B :] -= dg(left, right, 0, 0)
    store.start()
    corner = split(inverse.T)
    if p > 0:
        above = dot3s((xh_ref[:o, :o], xl_ref[:o, :o]), (uh_ref[:o, o:e], ul_ref[:o, o:e]))
        xh_ref[:o, o:e], xl_ref[:o, o:e] = split(-dot3s(split(above), corner))
    xh_ref[o:e, o:e], xl_ref[o:e, o:e] = corner
    if e < COLS:
        xh_ref[e:, o:e] = jnp.zeros((COLS - e, B), bf16)
        xl_ref[e:, o:e] = jnp.zeros((COLS - e, B), bf16)
    if p == 1:
        load.wait()
    if p % 2:
        pair = slice(o - B, e)
        w = dg(f_ref[:, :e], xh_ref[:e, pair], 1, 0) + dg(f_ref[:, :e], xl_ref[:e, pair], 1, 0)
        acc_ref[...] += w * w


def factor_kernel(
    sample_ref, mine_ref, other_ref, got_ref, f_hbm, u_hbm, lev_hbm, sk_hbm,
    a_ref, s_ref, uh_ref, ul_ref, xh_ref, xl_ref, acc_ref, f_ref, u_ref, lev_ref, sk_ref, sem, u_sem,
):
    load = pltpu.make_async_copy(f_hbm, f_ref, sem.at[0])
    load.start()
    core = lax.axis_index("rows") % 2
    for k in range(SAMPLES // DEVICES):
        q = (sample_ref[k] & (ROWS_DEV - 1)) // GROUP
        spot = jnp.bitwise_xor(q % 2, core)
        row = got_ref[q // 2, pl.ds(pl.multiple_of(SHARE + spot * GROUP, GROUP), GROUP), :]
        for b in range(NB):
            sk_ref[k : k + 1, b * B : (b + 1) * B] = row[b : b + 1, :]
    rows_out = pltpu.make_async_copy(sk_ref, sk_hbm, sem.at[1])
    rows_out.start()
    first = core == 0
    for r in range(NB):
        for c in range(r, NB):
            half, spot = divmod(tile_index(r, c), HALF_TILES)
            own = mine_ref[spot * B : (spot + 1) * B, :]
            far = other_ref[spot * B : (spot + 1) * B, :]
            a_ref[r * B : (r + 1) * B, c * B : (c + 1) * B] = jnp.where(first == (half == 0), own, far)
    u_ref[...] = jnp.zeros_like(u_ref)
    acc_ref[...] = jnp.zeros_like(acc_ref)
    ri = lax.broadcasted_iota(jnp.int32, (B, B), 0)
    ci = lax.broadcasted_iota(jnp.int32, (B, B), 1)

    def store(p):
        rows = pl.ds(p * B, B)
        return pltpu.make_async_copy(u_ref.at[rows, :], u_hbm.at[rows, :], u_sem.at[p])

    def panel(p, _):
        o = pl.multiple_of(p * B, B)
        s_ref[:, :B] = a_ref[pl.ds(o, B), pl.ds(o, B)]
        s_ref[:, B:] = jnp.where(ri == ci, 1.0, 0.0).astype(f32)
        for i in range(B // SB):
            factor_rows(s_ref, i)
            if i < B // SB - 1:
                R = s_ref[i * SB : (i + 1) * SB, :]
                update = dot3(R[:, :B], R, 0, 0)
                s_ref[(i + 1) * SB :, :] = s_ref[(i + 1) * SB :, :] - update[(i + 1) * SB :, :]
        for static in range(NB):

            @pl.when(p == static)
            def _():
                finish_panel(static, load, store(static), f_ref, u_ref, a_ref, s_ref, uh_ref, ul_ref, xh_ref, xl_ref, acc_ref)

        return 0

    lax.fori_loop(0, NB, panel, 0)
    high, low = split(acc_ref[...])
    weight = jnp.full((8, 2 * B), float(DEVICES * ROWS_DEV // COLS), bf16)
    lev_ref[...] = (dg(weight, high, 1, 1) + dg(weight, low, 1, 1))[:1, :]
    lev_out = pltpu.make_async_copy(lev_ref, lev_hbm, sem.at[2])
    lev_out.start()
    rows_out.wait()
    for p in range(NB):
        store(p).wait()
    lev_out.wait()


def factor(sample_rows, mine, other, got, features):
    samples = SAMPLES // DEVICES
    return pl.pallas_call(
        factor_kernel,
        out_shape=(
            jax.ShapeDtypeStruct((COLS, COLS), f32),
            jax.ShapeDtypeStruct((1, ROWS_DEV), f32),
            jax.ShapeDtypeStruct((samples, COLS), f32),
        ),
        in_specs=[SMEM, VMEM, VMEM, VMEM, ANY],
        out_specs=(ANY,) * 3,
        scratch_shapes=[pltpu.VMEM((COLS, COLS), f32), pltpu.VMEM((B, 2 * B), f32)]
        + [pltpu.VMEM((COLS, COLS), bf16)] * 4
        + [
            pltpu.VMEM((ROWS_DEV, 2 * B), f32),
            pltpu.VMEM((ROWS_DEV, COLS), bf16),
            pltpu.VMEM((COLS, COLS), f32),
            pltpu.VMEM((1, ROWS_DEV), f32),
            pltpu.VMEM((samples, COLS), f32),
            pltpu.SemaphoreType.DMA((3,)),
            pltpu.SemaphoreType.DMA((NB,)),
        ],
        compiler_params=pltpu.CompilerParams(vmem_limit_bytes=32 << 20),
        name="factor",
    )(sample_rows, mine, other, got, features)


def shards(features, flip_signs, sample_rows):
    mixed = transform(features, flip_signs, sample_rows)
    pieces = lax.all_to_all(
        mixed.reshape(DEVICES, GROUP, COLS + B), "rows", split_axis=0, concat_axis=0, tiled=True
    ).reshape(ROWS_DEV, COLS + B)
    mine, other = combine(pieces)
    swap = [(d, d ^ 1) for d in range(DEVICES)]
    came = lax.ppermute(other, "rows", swap).reshape(CHIPS, CHUNK, B)
    mine = mine.reshape(CHIPS, CHUNK, B)
    shares = jnp.concatenate([mine[:, :SHARE] + came[:, :SHARE], mine[:, SHARE:], came[:, SHARE:]], axis=1)
    same_core = [list(range(c, DEVICES, 2)) for c in range(2)]
    got = lax.all_to_all(
        shares, "rows", split_axis=0, concat_axis=0, tiled=True, axis_index_groups=same_core
    )
    total = jnp.sum(got[:, :SHARE], axis=0)
    half = lax.all_to_all(
        jnp.broadcast_to(total[None], (CHIPS, SHARE, B)),
        "rows", split_axis=0, concat_axis=0, tiled=True, axis_index_groups=same_core,
    ).reshape(HALF_TILES * B, B)
    far = lax.ppermute(half, "rows", swap)
    upper, lev, sketch = factor(sample_rows, half, far, got, features)
    return sketch, upper, lev.reshape(-1)


def solution(mesh):
    placed = (P("rows", None), P("rows"), P("rows"))
    return jax.shard_map(
        shards,
        mesh=mesh,
        in_specs=placed,
        out_specs=(P("rows", None), P(), P("rows")),
        check_vma=False,
    )
```

```python
import math

import jax
import jax.numpy as jnp
from jax import lax
from jax.experimental import pallas as pl
from jax.experimental.pallas import tpu as pltpu
from jax.sharding import PartitionSpec as P

FACTOR = 128
SAMPLES = 4096
COLS = 1024
ROWS_DEV = 1024
GROUP = 8
DEVICES = 128
CHIPS = 64
B = 128
NB = COLS // B
SB = 64
HALF_TILES = 20
SHARE = HALF_TILES * B // CHIPS
CHUNK = SHARE + GROUP
f32 = jnp.float32
bf16 = jnp.bfloat16
ANY = pl.BlockSpec(memory_space=pl.ANY)
HBM = pl.BlockSpec(memory_space=pltpu.HBM)
VMEM = pl.BlockSpec(memory_space=pltpu.VMEM)
SMEM = pl.BlockSpec(memory_space=pltpu.SMEM)


def tile_index(row, col):
    return row * NB - row * (row - 1) // 2 + col - row


def dg(a, b, ca, cb):
    return lax.dot_general(a, b, (((ca,), (cb,)), ((), ())), preferred_element_type=f32)


def split(x):
    high = x.astype(bf16)
    return high, (x - high.astype(f32)).astype(bf16)


def dot3(a, b, ca=1, cb=0):
    (ah, al), (bh, bl) = a, b
    return dg(ah, bh, ca, cb) + dg(ah, bl, ca, cb) + dg(al, bh, ca, cb)


def iota(shape, dim):
    return lax.broadcasted_iota(jnp.int32, shape, dim)


def hadamard(rows, cols):
    bits = rows & cols
    for shift in (4, 2, 1):
        bits = bits ^ (bits >> shift)
    return (1 - 2 * (bits & 1)).astype(f32)


def transform_kernel(x_hbm, sign_hbm, rows_hbm, out_hbm, x_ref, out_ref, sign_ref, rows_ref, in_sem, out_sem, sem):
    blocks = ROWS_DEV // FACTOR
    width = 256
    parts = COLS // width

    def fetch(c):
        lanes = pl.ds(c * width, width)
        return pltpu.make_async_copy(x_hbm.at[:, lanes], x_ref.at[:, lanes], in_sem.at[c])

    def put(c):
        lanes = pl.ds(c * width, width) if c < parts else pl.ds(COLS, B)
        return pltpu.make_async_copy(out_ref.at[:, lanes], out_hbm.at[:, lanes], out_sem.at[c])

    sign_in = pltpu.make_async_copy(sign_hbm, sign_ref, sem.at[0])
    rows_in = pltpu.make_async_copy(rows_hbm, rows_ref, sem.at[1])
    rows_in.start()
    sign_in.start()
    for c in range(parts):
        fetch(c).start()
    square = (FACTOR, FACTOR)
    table = hadamard(iota(square, 0), iota(square, 1))
    rows_in.wait()
    sampled = rows_ref[...] & (ROWS_DEV - 1)
    ones = jnp.ones((sampled.shape[1], B), bf16)
    for start in range(0, ROWS_DEV, 256):
        place = lax.broadcasted_iota(jnp.int32, (256, sampled.shape[1]), 0) + start
        hit = jnp.where(place == sampled, 1.0, 0.0).astype(bf16)
        out_ref[start : start + 256, COLS:] = dg(hit, ones, 1, 0).astype(bf16)
    put(parts).start()
    sign_in.wait()
    signs = sign_ref[...].astype(f32)
    tables = [(table * signs[b : b + 1, :]).astype(bf16) for b in range(blocks)]
    for c in range(parts):
        fetch(c).wait()
        lanes = slice(c * width, (c + 1) * width)
        mixed = []
        for b in range(blocks):
            inner = dg(tables[b], x_ref[b * FACTOR : (b + 1) * FACTOR, lanes], 1, 0)
            mixed.append(inner.astype(bf16).astype(f32))
        step = 1
        while step < blocks:
            mixed = [
                mixed[b] + mixed[b ^ step] if not b & step else mixed[b ^ step] - mixed[b]
                for b in range(blocks)
            ]
            step *= 2
        for b in range(blocks):
            out_ref[b * FACTOR : (b + 1) * FACTOR, lanes] = mixed[b].astype(bf16)
        put(c).start()
    for c in range(parts + 1):
        put(c).wait()


def transform(features, flip_signs, sample_rows):
    parts = COLS // 256
    return pl.pallas_call(
        transform_kernel,
        out_shape=jax.ShapeDtypeStruct((ROWS_DEV, COLS + B), bf16),
        in_specs=[HBM] * 3,
        out_specs=ANY,
        scratch_shapes=[
            pltpu.VMEM((ROWS_DEV, COLS), bf16),
            pltpu.VMEM((ROWS_DEV, COLS + B), bf16),
            pltpu.VMEM((ROWS_DEV // FACTOR, FACTOR), jnp.int32),
            pltpu.VMEM((1, SAMPLES // DEVICES), jnp.int32),
            pltpu.SemaphoreType.DMA((parts,)),
            pltpu.SemaphoreType.DMA((parts + 1,)),
            pltpu.SemaphoreType.DMA((2,)),
        ],
        compiler_params=pltpu.CompilerParams(vmem_limit_bytes=16 << 20),
        name="transform",
    )(
        features,
        flip_signs.reshape(ROWS_DEV // FACTOR, FACTOR),
        sample_rows.reshape(1, -1),
    )


def combine_kernel(p_ref, mine_ref, other_ref, x_ref):
    core = lax.axis_index("rows") % 2
    mask = p_ref[:, COLS:].astype(f32)
    row = lax.broadcasted_iota(jnp.int32, (ROWS_DEV, B), 0)
    lane = lax.broadcasted_iota(jnp.int32, (ROWS_DEV, B), 1)
    mask = jnp.where((row & (GROUP - 1)) == (lane & (GROUP - 1)), mask, 0.0).astype(bf16)
    shape = (DEVICES, DEVICES * GROUP)
    place = iota(shape, 0)
    target = 2 * (place & (CHIPS - 1)) + place // CHIPS
    source = iota(shape, 1) // GROUP
    block = jnp.where(target == source, 1.0, 0.0).astype(bf16)
    pick = dg(block, mask, 1, 0)
    mixer = (hadamard(target, source) * jnp.concatenate([pick] * GROUP, axis=1)).astype(bf16)
    rows = dg(mixer, p_ref[:, :COLS], 1, 0) * (1.0 / math.sqrt(SAMPLES))
    for b in range(NB):
        for half in range(2):
            x_ref[pl.ds(half * CHIPS * CHUNK + SHARE + b, CHIPS, stride=CHUNK), :] = rows[
                half * CHIPS : (half + 1) * CHIPS, b * B : (b + 1) * B
            ]
    high, low = split(rows)
    for r in range(NB):
        left_high, left_low = high[:, r * B : (r + 1) * B], low[:, r * B : (r + 1) * B]
        right_high, right_low = high[:, r * B :], low[:, r * B :]
        gram = dg(left_high, right_high, 0, 0) + dg(left_high, right_low, 0, 0) + dg(left_low, right_high, 0, 0)
        for c in range(r, NB):
            half, spot = divmod(tile_index(r, c), HALF_TILES)
            tile = gram[:, (c - r) * B : (c - r + 1) * B]
            put_rows(x_ref, half, spot * B, tile)
    for t in range(NB * (NB + 1) // 2, 2 * HALF_TILES):
        half, spot = divmod(t, HALF_TILES)
        put_rows(x_ref, half, spot * B, jnp.zeros((B, B), f32))
    size = CHIPS * CHUNK
    mine_ref[...] = x_ref[pl.ds(pl.multiple_of(core * size, 8), size), :]
    other_ref[...] = x_ref[pl.ds(pl.multiple_of((1 - core) * size, 8), size), :]


def put_rows(x_ref, half, start, tile):
    done = 0
    while done < B:
        chip, spot = divmod(start + done, SHARE)
        count = min(SHARE - spot, B - done)
        base = (half * CHIPS + chip) * CHUNK + spot
        x_ref[base : base + count, :] = tile[done : done + count, :]
        done += count


def combine(pieces):
    shape = jax.ShapeDtypeStruct((CHIPS * CHUNK, B), f32)
    return pl.pallas_call(
        combine_kernel,
        out_shape=(shape, shape),
        in_specs=[VMEM],
        out_specs=(VMEM, VMEM),
        scratch_shapes=[pltpu.VMEM((2 * CHIPS * CHUNK, B), f32)],
        compiler_params=pltpu.CompilerParams(vmem_limit_bytes=24 << 20),
        name="combine",
    )(pieces)


def factor_rows(s_ref, i):
    groups = SB // 8
    rid = lax.broadcasted_iota(jnp.int32, (8, B), 0)
    base = i * SB
    R = [[s_ref[base + 8 * v : base + 8 * v + 8, h * B : (h + 1) * B] for h in range(2)] for v in range(groups)]

    def spread(x, k):
        return jnp.broadcast_to(x[k : k + 1, :], (8, B))

    for g in range(groups):
        lane = base + 8 * g
        rest = range(groups - g)
        C = [[jnp.take_along_axis(R[g + v][0], jnp.full((8, B), lane + k, jnp.int32), axis=1) for v in rest] for k in range(8)]
        scale = None
        for k in range(8):
            pivot = spread(C[k][0], k)
            inverse = 1.0 / pivot
            factors = [C[k][v] * inverse for v in rest]
            factors[0] = jnp.where(rid > k, factors[0], 0.0)
            for j in range(k + 1, 8):
                row = spread(C[j][0], k)
                for v in rest:
                    C[j][v] = C[j][v] - factors[v] * row
            for h in range(2):
                row = spread(R[g][h], k)
                for v in rest:
                    R[g + v][h] = R[g + v][h] - factors[v] * row
            root = lax.rsqrt(pivot)
            scale = root if scale is None else jnp.where(rid >= k, root, scale)
        for h in range(2):
            R[g][h] = R[g][h] * scale
    for v in range(groups):
        for h in range(2):
            s_ref[base + 8 * v : base + 8 * v + 8, h * B : (h + 1) * B] = R[v][h]


def finish_panel(p, load, store, f_ref, u_ref, a_ref, s_ref, uh_ref, ul_ref, xh_ref, xl_ref, acc_ref):
    o = p * B
    e = o + B
    ri = lax.broadcasted_iota(jnp.int32, (B, B), 0)
    ci = lax.broadcasted_iota(jnp.int32, (B, B), 1)
    inverse = jnp.where(ri >= ci, s_ref[:, B:], 0.0)
    u_ref[o:e, o:e] = jnp.where(ri <= ci, s_ref[:, :B], 0.0)
    if e < COLS:
        across = dot3(split(inverse), split(a_ref[o:e, e:]))
        u_ref[o:e, e:] = across
        high, low = split(across)
        uh_ref[o:e, e:] = high
        ul_ref[o:e, e:] = low
        for q in range(p + 1, NB):
            c = q * B - e
            left = jnp.concatenate([high[:, c : c + B], high[:, c : c + B], low[:, c : c + B]], axis=0)
            right = jnp.concatenate([high[:, c:], low[:, c:], high[:, c:]], axis=0)
            a_ref[q * B : (q + 1) * B, q * B :] -= dg(left, right, 0, 0)
    store.start()
    corner = split(inverse.T)
    if p > 0:
        above = dot3((xh_ref[:o, :o], xl_ref[:o, :o]), (uh_ref[:o, o:e], ul_ref[:o, o:e]))
        xh_ref[:o, o:e], xl_ref[:o, o:e] = split(-dot3(split(above), corner))
    xh_ref[o:e, o:e], xl_ref[o:e, o:e] = corner
    if e < COLS:
        xh_ref[e:, o:e] = jnp.zeros((COLS - e, B), bf16)
        xl_ref[e:, o:e] = jnp.zeros((COLS - e, B), bf16)
    if p == 1:
        load.wait()
    if p % 2:
        pair = slice(o - B, e)
        w = dg(f_ref[:, :e], xh_ref[:e, pair], 1, 0) + dg(f_ref[:, :e], xl_ref[:e, pair], 1, 0)
        acc_ref[...] += w * w


def factor_kernel(
    sample_ref, mine_ref, other_ref, got_ref, f_hbm, u_hbm, lev_hbm, sk_hbm,
    a_ref, panels_ref, uh_ref, ul_ref, xh_ref, xl_ref, acc_ref, f_ref, u_ref, lev_ref, sk_ref, sem, u_sem,
):
    load = pltpu.make_async_copy(f_hbm, f_ref, sem.at[0])
    load.start()
    core = lax.axis_index("rows") % 2
    for k in range(SAMPLES // DEVICES):
        q = (sample_ref[k] & (ROWS_DEV - 1)) // GROUP
        spot = jnp.bitwise_xor(q % 2, core)
        row = got_ref[q // 2, pl.ds(pl.multiple_of(SHARE + spot * GROUP, GROUP), GROUP), :]
        for b in range(NB):
            sk_ref[k : k + 1, b * B : (b + 1) * B] = row[b : b + 1, :]
    rows_out = pltpu.make_async_copy(sk_ref, sk_hbm, sem.at[1])
    rows_out.start()
    first = core == 0
    for r in range(NB):
        for c in range(r, NB):
            half, spot = divmod(tile_index(r, c), HALF_TILES)
            own = mine_ref[spot * B : (spot + 1) * B, :]
            far = other_ref[spot * B : (spot + 1) * B, :]
            a_ref[r * B : (r + 1) * B, c * B : (c + 1) * B] = jnp.where(first == (half == 0), own, far)
    u_ref[...] = jnp.zeros_like(u_ref)
    acc_ref[...] = jnp.zeros_like(acc_ref)
    ri = lax.broadcasted_iota(jnp.int32, (B, B), 0)
    ci = lax.broadcasted_iota(jnp.int32, (B, B), 1)

    def store(p):
        rows = pl.ds(p * B, B)
        return pltpu.make_async_copy(u_ref.at[rows, :], u_hbm.at[rows, :], u_sem.at[p])

    for p in range(NB):
        o = p * B
        s_ref = panels_ref.at[p % 2]
        s_ref[:, :B] = a_ref[o : o + B, o : o + B]
        s_ref[:, B:] = jnp.where(ri == ci, 1.0, 0.0).astype(f32)
        for i in range(B // SB):
            factor_rows(s_ref, i)
            done = (i + 1) * SB
            if done < B:
                high, low = split(s_ref[i * SB : done, :])
                left = jnp.concatenate([high[:, :B], high[:, :B], low[:, :B]], axis=0)
                right = jnp.concatenate([high, low, high], axis=0)
                s_ref[done:, :] = s_ref[done:, :] - dg(left, right, 0, 0)[done:]
        finish_panel(p, load, store(p), f_ref, u_ref, a_ref, s_ref, uh_ref, ul_ref, xh_ref, xl_ref, acc_ref)
    high, low = split(acc_ref[...])
    weight = jnp.full((8, 2 * B), float(DEVICES * ROWS_DEV // COLS), bf16)
    lev_ref[...] = (dg(weight, high, 1, 1) + dg(weight, low, 1, 1))[:1, :]
    lev_out = pltpu.make_async_copy(lev_ref, lev_hbm, sem.at[2])
    lev_out.start()
    rows_out.wait()
    for p in range(NB):
        store(p).wait()
    lev_out.wait()


def factor(sample_rows, mine, other, got, features):
    samples = SAMPLES // DEVICES
    return pl.pallas_call(
        factor_kernel,
        out_shape=(
            jax.ShapeDtypeStruct((COLS, COLS), f32),
            jax.ShapeDtypeStruct((1, ROWS_DEV), f32),
            jax.ShapeDtypeStruct((samples, COLS), f32),
        ),
        in_specs=[SMEM, VMEM, VMEM, VMEM, ANY],
        out_specs=(ANY,) * 3,
        scratch_shapes=[pltpu.VMEM((COLS, COLS), f32), pltpu.VMEM((2, B, 2 * B), f32)]
        + [pltpu.VMEM((COLS, COLS), bf16)] * 4
        + [
            pltpu.VMEM((ROWS_DEV, 2 * B), f32),
            pltpu.VMEM((ROWS_DEV, COLS), bf16),
            pltpu.VMEM((COLS, COLS), f32),
            pltpu.VMEM((1, ROWS_DEV), f32),
            pltpu.VMEM((samples, COLS), f32),
            pltpu.SemaphoreType.DMA((3,)),
            pltpu.SemaphoreType.DMA((NB,)),
        ],
        compiler_params=pltpu.CompilerParams(vmem_limit_bytes=32 << 20),
        name="factor",
    )(sample_rows, mine, other, got, features)


def shards(features, flip_signs, sample_rows):
    mixed = transform(features, flip_signs, sample_rows)
    pieces = lax.all_to_all(
        mixed.reshape(DEVICES, GROUP, COLS + B), "rows", split_axis=0, concat_axis=0, tiled=True
    ).reshape(ROWS_DEV, COLS + B)
    mine, other = combine(pieces)
    swap = [(d, d ^ 1) for d in range(DEVICES)]
    came = lax.ppermute(other, "rows", swap).reshape(CHIPS, CHUNK, B)
    mine = mine.reshape(CHIPS, CHUNK, B)
    shares = jnp.concatenate([mine[:, :SHARE] + came[:, :SHARE], mine[:, SHARE:], came[:, SHARE:]], axis=1)
    same_core = [list(range(c, DEVICES, 2)) for c in range(2)]
    got = lax.all_to_all(
        shares, "rows", split_axis=0, concat_axis=0, tiled=True, axis_index_groups=same_core
    )
    total = jnp.sum(got[:, :SHARE], axis=0)
    half = lax.all_to_all(
        jnp.broadcast_to(total[None], (CHIPS, SHARE, B)),
        "rows", split_axis=0, concat_axis=0, tiled=True, axis_index_groups=same_core,
    ).reshape(HALF_TILES * B, B)
    far = lax.ppermute(half, "rows", swap)
    upper, lev, sketch = factor(sample_rows, half, far, got, features)
    return sketch, upper, lev.reshape(-1)


def solution(mesh):
    placed = (P("rows", None), P("rows"), P("rows"))
    return jax.shard_map(
        shards,
        mesh=mesh,
        in_specs=placed,
        out_specs=(P("rows", None), P(), P("rows")),
        check_vma=False,
    )
```

```python
import math

import jax
import jax.numpy as jnp
from jax import lax
from jax.experimental import pallas as pl
from jax.experimental.pallas import tpu as pltpu
from jax.sharding import PartitionSpec as P

FACTOR = 128
SAMPLES = 4096
COLS = 1024
ROWS_DEV = 1024
GROUP = 8
DEVICES = 128
CHIPS = 64
B = 128
NB = COLS // B
SB = 64
HALF_TILES = 20
SHARE = HALF_TILES * B // CHIPS
CHUNK = SHARE + 2 * GROUP
f32 = jnp.float32
bf16 = jnp.bfloat16
ANY = pl.BlockSpec(memory_space=pl.ANY)
HBM = pl.BlockSpec(memory_space=pltpu.HBM)
VMEM = pl.BlockSpec(memory_space=pltpu.VMEM)
SMEM = pl.BlockSpec(memory_space=pltpu.SMEM)


def tile_index(row, col):
    return row * NB - row * (row - 1) // 2 + col - row


def dg(a, b, ca, cb):
    return lax.dot_general(a, b, (((ca,), (cb,)), ((), ())), preferred_element_type=f32)


def split(x):
    high = x.astype(bf16)
    return high, (x - high.astype(f32)).astype(bf16)


def dot3(a, b, ca=1, cb=0):
    (ah, al), (bh, bl) = a, b
    return dg(ah, bh, ca, cb) + dg(ah, bl, ca, cb) + dg(al, bh, ca, cb)


def iota(shape, dim):
    return lax.broadcasted_iota(jnp.int32, shape, dim)


def hadamard(rows, cols):
    bits = rows & cols
    for shift in (4, 2, 1):
        bits = bits ^ (bits >> shift)
    return (1 - 2 * (bits & 1)).astype(f32)


def transform_kernel(x_hbm, sign_hbm, rows_hbm, out_hbm, x_ref, out_ref, sign_ref, rows_ref, in_sem, out_sem, sem):
    blocks = ROWS_DEV // FACTOR
    width = 256
    parts = COLS // width

    def fetch(c):
        lanes = pl.ds(c * width, width)
        return pltpu.make_async_copy(x_hbm.at[:, lanes], x_ref.at[:, lanes], in_sem.at[c])

    def put(c):
        lanes = pl.ds(c * width, width) if c < parts else pl.ds(COLS, B)
        return pltpu.make_async_copy(out_ref.at[:, lanes], out_hbm.at[:, lanes], out_sem.at[c])

    sign_in = pltpu.make_async_copy(sign_hbm, sign_ref, sem.at[0])
    rows_in = pltpu.make_async_copy(rows_hbm, rows_ref, sem.at[1])
    rows_in.start()
    sign_in.start()
    for c in range(parts):
        fetch(c).start()
    square = (FACTOR, FACTOR)
    table = hadamard(iota(square, 0), iota(square, 1))
    rows_in.wait()
    sampled = rows_ref[...] & (ROWS_DEV - 1)
    ones = jnp.ones((sampled.shape[1], B), bf16)
    for start in range(0, ROWS_DEV, 256):
        place = lax.broadcasted_iota(jnp.int32, (256, sampled.shape[1]), 0) + start
        hit = jnp.where(place == sampled, 1.0, 0.0).astype(bf16)
        out_ref[start : start + 256, COLS:] = dg(hit, ones, 1, 0).astype(bf16)
    put(parts).start()
    sign_in.wait()
    signs = sign_ref[...].astype(f32)
    tables = [(table * signs[b : b + 1, :]).astype(bf16) for b in range(blocks)]
    for c in range(parts):
        fetch(c).wait()
        lanes = slice(c * width, (c + 1) * width)
        mixed = []
        for b in range(blocks):
            inner = dg(tables[b], x_ref[b * FACTOR : (b + 1) * FACTOR, lanes], 1, 0)
            mixed.append(inner.astype(bf16).astype(f32))
        step = 1
        while step < blocks:
            mixed = [
                mixed[b] + mixed[b ^ step] if not b & step else mixed[b ^ step] - mixed[b]
                for b in range(blocks)
            ]
            step *= 2
        for b in range(blocks):
            out_ref[b * FACTOR : (b + 1) * FACTOR, lanes] = mixed[b].astype(bf16)
        put(c).start()
    for c in range(parts + 1):
        put(c).wait()


def transform(features, flip_signs, sample_rows):
    parts = COLS // 256
    return pl.pallas_call(
        transform_kernel,
        out_shape=jax.ShapeDtypeStruct((ROWS_DEV, COLS + B), bf16),
        in_specs=[HBM] * 3,
        out_specs=ANY,
        scratch_shapes=[
            pltpu.VMEM((ROWS_DEV, COLS), bf16),
            pltpu.VMEM((ROWS_DEV, COLS + B), bf16),
            pltpu.VMEM((ROWS_DEV // FACTOR, FACTOR), jnp.int32),
            pltpu.VMEM((1, SAMPLES // DEVICES), jnp.int32),
            pltpu.SemaphoreType.DMA((parts,)),
            pltpu.SemaphoreType.DMA((parts + 1,)),
            pltpu.SemaphoreType.DMA((2,)),
        ],
        compiler_params=pltpu.CompilerParams(vmem_limit_bytes=60 << 20),
        name="transform",
    )(
        features,
        flip_signs.reshape(ROWS_DEV // FACTOR, FACTOR),
        sample_rows.reshape(1, -1),
    )


def select_kernel(p_ref, rows_ref):
    mask = p_ref[:, COLS:].astype(f32)
    row = iota((ROWS_DEV, B), 0)
    lane = iota((ROWS_DEV, B), 1)
    mask = jnp.where((row & (GROUP - 1)) == (lane & (GROUP - 1)), mask, 0.0).astype(bf16)
    shape = (DEVICES, DEVICES * GROUP)
    place = iota(shape, 0)
    target = 2 * (place & (CHIPS - 1)) + place // CHIPS
    source = iota(shape, 1) // GROUP
    block = jnp.where(target == source, 1.0, 0.0).astype(bf16)
    pick = dg(block, mask, 1, 0)
    mixer = (hadamard(target, source) * jnp.concatenate([pick] * GROUP, axis=1)).astype(bf16)
    rows_ref[...] = dg(mixer, p_ref[:, :COLS], 1, 0) * (1.0 / math.sqrt(SAMPLES))


def select(pieces):
    return pl.pallas_call(
        select_kernel,
        out_shape=jax.ShapeDtypeStruct((DEVICES, COLS), f32),
        in_specs=[VMEM],
        out_specs=VMEM,
        compiler_params=pltpu.CompilerParams(vmem_limit_bytes=24 << 20),
        name="select",
    )(pieces)


def put_rows(x_ref, start, tile):
    done = 0
    while done < B:
        chip, spot = divmod(start + done, SHARE)
        count = min(SHARE - spot, B - done)
        base = chip * CHUNK + spot
        x_ref[base : base + count, :] = tile[done : done + count, :]
        done += count


def gram_kernel(mine_ref, came_ref, x_ref, high_ref, low_ref):
    core = lax.axis_index("rows") % 2
    for j, ref in enumerate((mine_ref, came_ref)):
        owned = ref[pl.ds(pl.multiple_of(core * CHIPS, CHIPS), CHIPS), :]
        for b in range(NB):
            x_ref[pl.ds(SHARE + GROUP * j + b, CHIPS, stride=CHUNK), :] = owned[:, b * B : (b + 1) * B]
        high, low = split(ref[...])
        high_ref[j * DEVICES : (j + 1) * DEVICES, :] = high
        low_ref[j * DEVICES : (j + 1) * DEVICES, :] = low
    count = NB * (NB + 1) // 2
    for half in range(2):

        @pl.when(core == half)
        def _():
            for r in range(NB):
                inside = [
                    c for c in range(r, NB) if half * HALF_TILES <= tile_index(r, c) < (half + 1) * HALF_TILES
                ]
                if not inside:
                    continue
                left = slice(r * B, (r + 1) * B)
                right = slice(inside[0] * B, (inside[-1] + 1) * B)
                gram = dot3((high_ref[:, left], low_ref[:, left]), (high_ref[:, right], low_ref[:, right]), 0, 0)
                for n, c in enumerate(inside):
                    put_rows(x_ref, (tile_index(r, c) - half * HALF_TILES) * B, gram[:, n * B : (n + 1) * B])
            for t in range(count - half * HALF_TILES, HALF_TILES):
                put_rows(x_ref, t * B, jnp.zeros((B, B), f32))


def gram_share(mine, came):
    return pl.pallas_call(
        gram_kernel,
        out_shape=jax.ShapeDtypeStruct((CHIPS * CHUNK, B), f32),
        in_specs=[VMEM, VMEM],
        out_specs=VMEM,
        scratch_shapes=[pltpu.VMEM((2 * DEVICES, COLS), bf16)] * 2,
        compiler_params=pltpu.CompilerParams(vmem_limit_bytes=24 << 20),
        name="gram",
    )(mine, came)


def factor_rows(s_ref, i):
    groups = SB // 8
    rid = lax.broadcasted_iota(jnp.int32, (8, B), 0)
    base = i * SB
    R = [[s_ref[base + 8 * v : base + 8 * v + 8, h * B : (h + 1) * B] for h in range(2)] for v in range(groups)]

    def spread(x, k):
        return jnp.broadcast_to(x[k : k + 1, :], (8, B))

    for g in range(groups):
        lane = base + 8 * g
        rest = range(groups - g)
        C = [[jnp.take_along_axis(R[g + v][0], jnp.full((8, B), lane + k, jnp.int32), axis=1) for v in rest] for k in range(8)]
        scale = None
        for k in range(8):
            pivot = spread(C[k][0], k)
            inverse = 1.0 / pivot
            factors = [C[k][v] * inverse for v in rest]
            factors[0] = jnp.where(rid > k, factors[0], 0.0)
            for j in range(k + 1, 8):
                row = spread(C[j][0], k)
                for v in rest:
                    C[j][v] = C[j][v] - factors[v] * row
            for h in range(2):
                row = spread(R[g][h], k)
                for v in rest:
                    R[g + v][h] = R[g + v][h] - factors[v] * row
            root = lax.rsqrt(pivot)
            scale = root if scale is None else jnp.where(rid >= k, root, scale)
        for h in range(2):
            R[g][h] = R[g][h] * scale
    for v in range(groups):
        for h in range(2):
            s_ref[base + 8 * v : base + 8 * v + 8, h * B : (h + 1) * B] = R[v][h]


def finish_panel(p, load, store, f_ref, u_ref, a_ref, s_ref, uh_ref, ul_ref, xh_ref, xl_ref, acc_ref):
    o = p * B
    e = o + B
    ri = lax.broadcasted_iota(jnp.int32, (B, B), 0)
    ci = lax.broadcasted_iota(jnp.int32, (B, B), 1)
    inverse = jnp.where(ri >= ci, s_ref[:, B:], 0.0)
    u_ref[o:e, o:e] = jnp.where(ri <= ci, s_ref[:, :B], 0.0)
    if e < COLS:
        across = dot3(split(inverse), split(a_ref[o:e, e:]))
        u_ref[o:e, e:] = across
        high, low = split(across)
        uh_ref[o:e, e:] = high
        ul_ref[o:e, e:] = low
        for q in range(p + 1, NB):
            c = q * B - e
            left = jnp.concatenate([high[:, c : c + B], high[:, c : c + B], low[:, c : c + B]], axis=0)
            right = jnp.concatenate([high[:, c:], low[:, c:], high[:, c:]], axis=0)
            a_ref[q * B : (q + 1) * B, q * B :] -= dg(left, right, 0, 0)
    store.start()
    corner = split(inverse.T)
    if p > 0:
        above = dot3((xh_ref[:o, :o], xl_ref[:o, :o]), (uh_ref[:o, o:e], ul_ref[:o, o:e]))
        xh_ref[:o, o:e], xl_ref[:o, o:e] = split(-dot3(split(above), corner))
    xh_ref[o:e, o:e], xl_ref[o:e, o:e] = corner
    if e < COLS:
        xh_ref[e:, o:e] = jnp.zeros((COLS - e, B), bf16)
        xl_ref[e:, o:e] = jnp.zeros((COLS - e, B), bf16)
    if p == 1:
        load.wait()
    if p % 2:
        pair = slice(o - B, e)
        w = dg(f_ref[:, :e], xh_ref[:e, pair], 1, 0) + dg(f_ref[:, :e], xl_ref[:e, pair], 1, 0)
        acc_ref[...] += w * w


def factor_kernel(
    sample_ref, mine_ref, other_ref, got_ref, f_hbm, u_hbm, lev_hbm, sk_hbm,
    a_ref, panels_ref, uh_ref, ul_ref, xh_ref, xl_ref, acc_ref, f_ref, u_ref, lev_ref, sk_ref, sem, u_sem,
):
    load = pltpu.make_async_copy(f_hbm, f_ref, sem.at[0])
    load.start()
    core = lax.axis_index("rows") % 2
    for k in range(SAMPLES // DEVICES):
        q = (sample_ref[k] & (ROWS_DEV - 1)) // GROUP
        spot = jnp.bitwise_xor(q % 2, core)
        row = got_ref[q // 2, pl.ds(pl.multiple_of(SHARE + spot * GROUP, GROUP), GROUP), :]
        for b in range(NB):
            sk_ref[k : k + 1, b * B : (b + 1) * B] = row[b : b + 1, :]
    rows_out = pltpu.make_async_copy(sk_ref, sk_hbm, sem.at[1])
    rows_out.start()
    first = core == 0
    for r in range(NB):
        for c in range(r, NB):
            half, spot = divmod(tile_index(r, c), HALF_TILES)
            own = mine_ref[spot * B : (spot + 1) * B, :]
            far = other_ref[spot * B : (spot + 1) * B, :]
            a_ref[r * B : (r + 1) * B, c * B : (c + 1) * B] = jnp.where(first == (half == 0), own, far)
    u_ref[...] = jnp.zeros_like(u_ref)
    acc_ref[...] = jnp.zeros_like(acc_ref)
    ri = lax.broadcasted_iota(jnp.int32, (B, B), 0)
    ci = lax.broadcasted_iota(jnp.int32, (B, B), 1)

    def store(p):
        rows = pl.ds(p * B, B)
        return pltpu.make_async_copy(u_ref.at[rows, :], u_hbm.at[rows, :], u_sem.at[p])

    for p in range(NB):
        o = p * B
        s_ref = panels_ref.at[p % 2]
        s_ref[:, :B] = a_ref[o : o + B, o : o + B]
        s_ref[:, B:] = jnp.where(ri == ci, 1.0, 0.0).astype(f32)
        for i in range(B // SB):
            factor_rows(s_ref, i)
            done = (i + 1) * SB
            if done < B:
                high, low = split(s_ref[i * SB : done, :])
                left = jnp.concatenate([high[:, :B], high[:, :B], low[:, :B]], axis=0)
                right = jnp.concatenate([high, low, high], axis=0)
                s_ref[done:, :] = s_ref[done:, :] - dg(left, right, 0, 0)[done:]
        finish_panel(p, load, store(p), f_ref, u_ref, a_ref, s_ref, uh_ref, ul_ref, xh_ref, xl_ref, acc_ref)
    high, low = split(acc_ref[...])
    weight = jnp.full((8, 2 * B), float(DEVICES * ROWS_DEV // COLS), bf16)
    lev_ref[...] = (dg(weight, high, 1, 1) + dg(weight, low, 1, 1))[:1, :]
    lev_out = pltpu.make_async_copy(lev_ref, lev_hbm, sem.at[2])
    lev_out.start()
    rows_out.wait()
    for p in range(NB):
        store(p).wait()
    lev_out.wait()


def factor(sample_rows, mine, other, got, features):
    samples = SAMPLES // DEVICES
    return pl.pallas_call(
        factor_kernel,
        out_shape=(
            jax.ShapeDtypeStruct((COLS, COLS), f32),
            jax.ShapeDtypeStruct((1, ROWS_DEV), f32),
            jax.ShapeDtypeStruct((samples, COLS), f32),
        ),
        in_specs=[SMEM, VMEM, VMEM, VMEM, ANY],
        out_specs=(ANY,) * 3,
        scratch_shapes=[pltpu.VMEM((COLS, COLS), f32), pltpu.VMEM((2, B, 2 * B), f32)]
        + [pltpu.VMEM((COLS, COLS), bf16)] * 4
        + [
            pltpu.VMEM((ROWS_DEV, 2 * B), f32),
            pltpu.VMEM((ROWS_DEV, COLS), bf16),
            pltpu.VMEM((COLS, COLS), f32),
            pltpu.VMEM((1, ROWS_DEV), f32),
            pltpu.VMEM((samples, COLS), f32),
            pltpu.SemaphoreType.DMA((3,)),
            pltpu.SemaphoreType.DMA((NB,)),
        ],
        compiler_params=pltpu.CompilerParams(vmem_limit_bytes=32 << 20),
        name="factor",
    )(sample_rows, mine, other, got, features)


def shards(features, flip_signs, sample_rows):
    mixed = transform(features, flip_signs, sample_rows)
    pieces = lax.all_to_all(
        mixed.reshape(DEVICES, GROUP, COLS + B), "rows", split_axis=0, concat_axis=0, tiled=True
    ).reshape(ROWS_DEV, COLS + B)
    swap = [(d, d ^ 1) for d in range(DEVICES)]
    rows = select(pieces)
    shares = gram_share(rows, lax.ppermute(rows, "rows", swap)).reshape(CHIPS, CHUNK, B)
    same_core = [list(range(c, DEVICES, 2)) for c in range(2)]
    got = lax.all_to_all(
        shares, "rows", split_axis=0, concat_axis=0, tiled=True, axis_index_groups=same_core
    )
    total = jnp.sum(got[:, :SHARE], axis=0)
    half = lax.all_to_all(
        jnp.broadcast_to(total[None], (CHIPS, SHARE, B)),
        "rows", split_axis=0, concat_axis=0, tiled=True, axis_index_groups=same_core,
    ).reshape(HALF_TILES * B, B)
    far = lax.ppermute(half, "rows", swap)
    upper, lev, sketch = factor(sample_rows, half, far, got, features)
    return sketch, upper, lev.reshape(-1)


def solution(mesh):
    placed = (P("rows", None), P("rows"), P("rows"))
    return jax.shard_map(
        shards,
        mesh=mesh,
        in_specs=placed,
        out_specs=(P("rows", None), P(), P("rows")),
        check_vma=False,
    )
```

```python
import math

import jax
import jax.numpy as jnp
from jax import lax
from jax.experimental import pallas as pl
from jax.experimental.pallas import tpu as pltpu
from jax.sharding import PartitionSpec as P

FACTOR = 128
SAMPLES = 4096
COLS = 1024
ROWS_DEV = 1024
GROUP = 8
DEVICES = 128
CHIPS = 64
B = 128
NB = COLS // B
SB = 64
HALF_TILES = 20
SHARE = HALF_TILES * B // CHIPS
CHUNK = SHARE + 2 * GROUP
f32 = jnp.float32
bf16 = jnp.bfloat16
ANY = pl.BlockSpec(memory_space=pl.ANY)
HBM = pl.BlockSpec(memory_space=pltpu.HBM)
VMEM = pl.BlockSpec(memory_space=pltpu.VMEM)
SMEM = pl.BlockSpec(memory_space=pltpu.SMEM)


def tile_index(row, col):
    return row * NB - row * (row - 1) // 2 + col - row


def dg(a, b, ca, cb):
    return lax.dot_general(a, b, (((ca,), (cb,)), ((), ())), preferred_element_type=f32)


def split(x):
    high = x.astype(bf16)
    return high, (x - high.astype(f32)).astype(bf16)


def dot3(a, b, ca=1, cb=0):
    (ah, al), (bh, bl) = a, b
    return dg(ah, bh, ca, cb) + dg(ah, bl, ca, cb) + dg(al, bh, ca, cb)


def iota(shape, dim):
    return lax.broadcasted_iota(jnp.int32, shape, dim)


def hadamard(rows, cols):
    bits = rows & cols
    for shift in (4, 2, 1):
        bits = bits ^ (bits >> shift)
    return (1 - 2 * (bits & 1)).astype(f32)


def transform_kernel(x_hbm, sign_hbm, rows_hbm, out_hbm, x_ref, out_ref, sign_ref, rows_ref, in_sem, out_sem, sem):
    blocks = ROWS_DEV // FACTOR
    width = 256
    parts = COLS // width

    def fetch(c):
        lanes = pl.ds(c * width, width)
        return pltpu.make_async_copy(x_hbm.at[:, lanes], x_ref.at[:, lanes], in_sem.at[c])

    def put(c):
        lanes = pl.ds(c * width, width) if c < parts else pl.ds(COLS, B)
        return pltpu.make_async_copy(out_ref.at[:, lanes], out_hbm.at[:, lanes], out_sem.at[c])

    sign_in = pltpu.make_async_copy(sign_hbm, sign_ref, sem.at[0])
    rows_in = pltpu.make_async_copy(rows_hbm, rows_ref, sem.at[1])
    rows_in.start()
    sign_in.start()
    for c in range(parts):
        fetch(c).start()
    square = (FACTOR, FACTOR)
    table = hadamard(iota(square, 0), iota(square, 1))
    rows_in.wait()
    sampled = rows_ref[...] & (ROWS_DEV - 1)
    ones = jnp.ones((sampled.shape[1], B), bf16)
    for start in range(0, ROWS_DEV, 256):
        place = lax.broadcasted_iota(jnp.int32, (256, sampled.shape[1]), 0) + start
        hit = jnp.where(place == sampled, 1.0, 0.0).astype(bf16)
        out_ref[start : start + 256, COLS:] = dg(hit, ones, 1, 0).astype(bf16)
    put(parts).start()
    sign_in.wait()
    signs = sign_ref[...].astype(f32)
    tables = [(table * signs[b : b + 1, :]).astype(bf16) for b in range(blocks)]
    for c in range(parts):
        fetch(c).wait()
        lanes = slice(c * width, (c + 1) * width)
        mixed = []
        for b in range(blocks):
            inner = dg(tables[b], x_ref[b * FACTOR : (b + 1) * FACTOR, lanes], 1, 0)
            mixed.append(inner.astype(bf16).astype(f32))
        step = 1
        while step < blocks:
            mixed = [
                mixed[b] + mixed[b ^ step] if not b & step else mixed[b ^ step] - mixed[b]
                for b in range(blocks)
            ]
            step *= 2
        for b in range(blocks):
            out_ref[b * FACTOR : (b + 1) * FACTOR, lanes] = mixed[b].astype(bf16)
        put(c).start()
    for c in range(parts + 1):
        put(c).wait()


def transform(features, flip_signs, sample_rows):
    parts = COLS // 256
    return pl.pallas_call(
        transform_kernel,
        out_shape=jax.ShapeDtypeStruct((ROWS_DEV, COLS + B), bf16),
        in_specs=[HBM] * 3,
        out_specs=ANY,
        scratch_shapes=[
            pltpu.VMEM((ROWS_DEV, COLS), bf16),
            pltpu.VMEM((ROWS_DEV, COLS + B), bf16),
            pltpu.VMEM((ROWS_DEV // FACTOR, FACTOR), jnp.int32),
            pltpu.VMEM((1, SAMPLES // DEVICES), jnp.int32),
            pltpu.SemaphoreType.DMA((parts,)),
            pltpu.SemaphoreType.DMA((parts + 1,)),
            pltpu.SemaphoreType.DMA((2,)),
        ],
        compiler_params=pltpu.CompilerParams(vmem_limit_bytes=60 << 20),
        name="transform",
    )(
        features,
        flip_signs.reshape(ROWS_DEV // FACTOR, FACTOR),
        sample_rows.reshape(1, -1),
    )


def select_kernel(p_ref, rows_ref):
    mask = p_ref[:, COLS:].astype(f32)
    row = iota((ROWS_DEV, B), 0)
    lane = iota((ROWS_DEV, B), 1)
    mask = jnp.where((row & (GROUP - 1)) == (lane & (GROUP - 1)), mask, 0.0).astype(bf16)
    shape = (DEVICES, DEVICES * GROUP)
    place = iota(shape, 0)
    target = 2 * (place & (CHIPS - 1)) + place // CHIPS
    source = iota(shape, 1) // GROUP
    block = jnp.where(target == source, 1.0, 0.0).astype(bf16)
    pick = dg(block, mask, 1, 0)
    mixer = (hadamard(target, source) * jnp.concatenate([pick] * GROUP, axis=1)).astype(bf16)
    rows_ref[...] = dg(mixer, p_ref[:, :COLS], 1, 0) * (1.0 / math.sqrt(SAMPLES))


def select(pieces):
    return pl.pallas_call(
        select_kernel,
        out_shape=jax.ShapeDtypeStruct((DEVICES, COLS), f32),
        in_specs=[VMEM],
        out_specs=VMEM,
        compiler_params=pltpu.CompilerParams(vmem_limit_bytes=24 << 20),
        name="select",
    )(pieces)


def put_rows(x_ref, start, tile):
    done = 0
    while done < B:
        chip, spot = divmod(start + done, SHARE)
        count = min(SHARE - spot, B - done)
        base = chip * CHUNK + spot
        x_ref[base : base + count, :] = tile[done : done + count, :]
        done += count


def gram_kernel(mine_ref, came_ref, x_ref, high_ref, low_ref):
    core = lax.axis_index("rows") % 2
    for j, ref in enumerate((mine_ref, came_ref)):
        owned = ref[pl.ds(pl.multiple_of(core * CHIPS, CHIPS), CHIPS), :]
        for b in range(NB):
            x_ref[pl.ds(SHARE + GROUP * j + b, CHIPS, stride=CHUNK), :] = owned[:, b * B : (b + 1) * B]
        high, low = split(ref[...])
        high_ref[j * DEVICES : (j + 1) * DEVICES, :] = high
        low_ref[j * DEVICES : (j + 1) * DEVICES, :] = low
    count = NB * (NB + 1) // 2
    for half in range(2):

        @pl.when(core == half)
        def _():
            for r in range(NB):
                inside = [
                    c for c in range(r, NB) if half * HALF_TILES <= tile_index(r, c) < (half + 1) * HALF_TILES
                ]
                if not inside:
                    continue
                left = slice(r * B, (r + 1) * B)
                right = slice(inside[0] * B, (inside[-1] + 1) * B)
                gram = dot3((high_ref[:, left], low_ref[:, left]), (high_ref[:, right], low_ref[:, right]), 0, 0)
                for n, c in enumerate(inside):
                    put_rows(x_ref, (tile_index(r, c) - half * HALF_TILES) * B, gram[:, n * B : (n + 1) * B])
            for t in range(count - half * HALF_TILES, HALF_TILES):
                put_rows(x_ref, t * B, jnp.zeros((B, B), f32))


def gram_share(mine, came):
    return pl.pallas_call(
        gram_kernel,
        out_shape=jax.ShapeDtypeStruct((CHIPS * CHUNK, B), f32),
        in_specs=[VMEM, VMEM],
        out_specs=VMEM,
        scratch_shapes=[pltpu.VMEM((2 * DEVICES, COLS), bf16)] * 2,
        compiler_params=pltpu.CompilerParams(vmem_limit_bytes=24 << 20),
        name="gram",
    )(mine, came)


def factor_rows(s_ref, i):
    groups = SB // 8
    rid = lax.broadcasted_iota(jnp.int32, (8, B), 0)
    base = i * SB
    R = [[s_ref[base + 8 * v : base + 8 * v + 8, h * B : (h + 1) * B] for h in range(2)] for v in range(groups)]

    def spread(x, k):
        return jnp.broadcast_to(x[k : k + 1, :], (8, B))

    for g in range(groups):
        lane = base + 8 * g
        rest = range(groups - g)
        C = [[jnp.take_along_axis(R[g + v][0], jnp.full((8, B), lane + k, jnp.int32), axis=1) for v in rest] for k in range(8)]
        scale = None
        for k in range(8):
            pivot = spread(C[k][0], k)
            inverse = 1.0 / pivot
            factors = [C[k][v] * inverse for v in rest]
            factors[0] = jnp.where(rid > k, factors[0], 0.0)
            for j in range(k + 1, 8):
                row = spread(C[j][0], k)
                for v in rest:
                    C[j][v] = C[j][v] - factors[v] * row
            for h in range(2):
                row = spread(R[g][h], k)
                for v in rest:
                    R[g + v][h] = R[g + v][h] - factors[v] * row
            root = lax.rsqrt(pivot)
            scale = root if scale is None else jnp.where(rid >= k, root, scale)
        for h in range(2):
            R[g][h] = R[g][h] * scale
    for v in range(groups):
        for h in range(2):
            s_ref[base + 8 * v : base + 8 * v + 8, h * B : (h + 1) * B] = R[v][h]


def finish_panel(p, load, store, f_ref, u_ref, a_ref, s_ref, uh_ref, ul_ref, xh_ref, xl_ref, acc_ref):
    o = p * B
    e = o + B
    ri = lax.broadcasted_iota(jnp.int32, (B, B), 0)
    ci = lax.broadcasted_iota(jnp.int32, (B, B), 1)
    inverse = jnp.where(ri >= ci, s_ref[:, B:], 0.0)
    u_ref[o:e, o:e] = jnp.where(ri <= ci, s_ref[:, :B], 0.0)
    if e < COLS:
        across = dot3(split(inverse), split(a_ref[o:e, e:]))
        u_ref[o:e, e:] = across
        high, low = split(across)
        uh_ref[o:e, e:] = high
        ul_ref[o:e, e:] = low
        for q in range(p + 1, NB):
            c = q * B - e
            left = jnp.concatenate([high[:, c : c + B], high[:, c : c + B], low[:, c : c + B]], axis=0)
            right = jnp.concatenate([high[:, c:], low[:, c:], high[:, c:]], axis=0)
            a_ref[q * B : (q + 1) * B, q * B :] -= dg(left, right, 0, 0)
    store.start()
    corner = split(inverse.T)
    if p > 0:
        above = dot3((xh_ref[:o, :o], xl_ref[:o, :o]), (uh_ref[:o, o:e], ul_ref[:o, o:e]))
        xh_ref[:o, o:e], xl_ref[:o, o:e] = split(-dot3(split(above), corner))
    xh_ref[o:e, o:e], xl_ref[o:e, o:e] = corner
    if e < COLS:
        xh_ref[e:, o:e] = jnp.zeros((COLS - e, B), bf16)
        xl_ref[e:, o:e] = jnp.zeros((COLS - e, B), bf16)
    if p == 1:
        load.wait()
    if p % 2:
        pair = slice(o - B, e)
        w = dg(f_ref[:, :e], xh_ref[:e, pair], 1, 0) + dg(f_ref[:, :e], xl_ref[:e, pair], 1, 0)
        acc_ref[...] = w * w if p == 1 else acc_ref[...] + w * w


def factor_kernel(
    sample_ref, mine_ref, other_ref, got_ref, f_hbm, u_hbm, lev_hbm, sk_hbm,
    a_ref, panels_ref, uh_ref, ul_ref, xh_ref, xl_ref, acc_ref, f_ref, u_ref, lev_ref, sk_ref, sem, u_sem,
):
    load = pltpu.make_async_copy(f_hbm, f_ref, sem.at[0])
    load.start()
    core = lax.axis_index("rows") % 2
    for k in range(SAMPLES // DEVICES):
        q = (sample_ref[k] & (ROWS_DEV - 1)) // GROUP
        spot = jnp.bitwise_xor(q % 2, core)
        row = got_ref[q // 2, pl.ds(pl.multiple_of(SHARE + spot * GROUP, GROUP), GROUP), :]
        for b in range(NB):
            sk_ref[k : k + 1, b * B : (b + 1) * B] = row[b : b + 1, :]
    rows_out = pltpu.make_async_copy(sk_ref, sk_hbm, sem.at[1])
    rows_out.start()
    first = core == 0
    for r in range(NB):
        for c in range(r, NB):
            half, spot = divmod(tile_index(r, c), HALF_TILES)
            own = mine_ref[spot * B : (spot + 1) * B, :]
            far = other_ref[spot * B : (spot + 1) * B, :]
            a_ref[r * B : (r + 1) * B, c * B : (c + 1) * B] = jnp.where(first == (half == 0), own, far)
    for r in range(1, NB):
        u_ref[r * B : (r + 1) * B, : r * B] = jnp.zeros((B, r * B), f32)
    ri = lax.broadcasted_iota(jnp.int32, (B, B), 0)
    ci = lax.broadcasted_iota(jnp.int32, (B, B), 1)

    def store(p):
        rows = pl.ds(p * B, B)
        return pltpu.make_async_copy(u_ref.at[rows, :], u_hbm.at[rows, :], u_sem.at[p])

    for p in range(NB):
        o = p * B
        s_ref = panels_ref.at[p % 2]
        s_ref[:, :B] = a_ref[o : o + B, o : o + B]
        s_ref[:, B:] = jnp.where(ri == ci, 1.0, 0.0).astype(f32)
        for i in range(B // SB):
            factor_rows(s_ref, i)
            done = (i + 1) * SB
            if done < B:
                high, low = split(s_ref[i * SB : done, :])
                left = jnp.concatenate([high[:, :B], high[:, :B], low[:, :B]], axis=0)
                right = jnp.concatenate([high, low, high], axis=0)
                s_ref[done:, :] = s_ref[done:, :] - dg(left, right, 0, 0)[done:]
        finish_panel(p, load, store(p), f_ref, u_ref, a_ref, s_ref, uh_ref, ul_ref, xh_ref, xl_ref, acc_ref)
    high, low = split(acc_ref[...])
    weight = jnp.full((8, 2 * B), float(DEVICES * ROWS_DEV // COLS), bf16)
    lev_ref[...] = (dg(weight, high, 1, 1) + dg(weight, low, 1, 1))[:1, :]
    lev_out = pltpu.make_async_copy(lev_ref, lev_hbm, sem.at[2])
    lev_out.start()
    rows_out.wait()
    for p in range(NB):
        store(p).wait()
    lev_out.wait()


def factor(sample_rows, mine, other, got, features):
    samples = SAMPLES // DEVICES
    return pl.pallas_call(
        factor_kernel,
        out_shape=(
            jax.ShapeDtypeStruct((COLS, COLS), f32),
            jax.ShapeDtypeStruct((1, ROWS_DEV), f32),
            jax.ShapeDtypeStruct((samples, COLS), f32),
        ),
        in_specs=[SMEM, VMEM, VMEM, VMEM, ANY],
        out_specs=(ANY,) * 3,
        scratch_shapes=[pltpu.VMEM((COLS, COLS), f32), pltpu.VMEM((2, B, 2 * B), f32)]
        + [pltpu.VMEM((COLS, COLS), bf16)] * 4
        + [
            pltpu.VMEM((ROWS_DEV, 2 * B), f32),
            pltpu.VMEM((ROWS_DEV, COLS), bf16),
            pltpu.VMEM((COLS, COLS), f32),
            pltpu.VMEM((1, ROWS_DEV), f32),
            pltpu.VMEM((samples, COLS), f32),
            pltpu.SemaphoreType.DMA((3,)),
            pltpu.SemaphoreType.DMA((NB,)),
        ],
        compiler_params=pltpu.CompilerParams(vmem_limit_bytes=32 << 20),
        name="factor",
    )(sample_rows, mine, other, got, features)


def shards(features, flip_signs, sample_rows):
    mixed = transform(features, flip_signs, sample_rows)
    pieces = lax.all_to_all(
        mixed.reshape(DEVICES, GROUP, COLS + B), "rows", split_axis=0, concat_axis=0, tiled=True
    ).reshape(ROWS_DEV, COLS + B)
    swap = [(d, d ^ 1) for d in range(DEVICES)]
    rows = select(pieces)
    shares = gram_share(rows, lax.ppermute(rows, "rows", swap)).reshape(CHIPS, CHUNK, B)
    same_core = [list(range(c, DEVICES, 2)) for c in range(2)]
    got = lax.all_to_all(
        shares, "rows", split_axis=0, concat_axis=0, tiled=True, axis_index_groups=same_core
    )
    total = jnp.sum(got[:, :SHARE], axis=0)
    half = lax.all_to_all(
        jnp.broadcast_to(total[None], (CHIPS, SHARE, B)),
        "rows", split_axis=0, concat_axis=0, tiled=True, axis_index_groups=same_core,
    ).reshape(HALF_TILES * B, B)
    far = lax.ppermute(half, "rows", swap)
    upper, lev, sketch = factor(sample_rows, half, far, got, features)
    return sketch, upper, lev.reshape(-1)


def solution(mesh):
    placed = (P("rows", None), P("rows"), P("rows"))
    return jax.shard_map(
        shards,
        mesh=mesh,
        in_specs=placed,
        out_specs=(P("rows", None), P(), P("rows")),
        check_vma=False,
    )
```
